32 devices in a mesh: band: 2 (over x), blk: 16 (over z, y, core).
Axes of the slice: x: 2, y: 2, z: 4, core: 2. Of those that a mesh axis runs over, the one named last changes fastest.
Arguments:
- spectra: bfloat16 [768, 4, 1024], P(('band', 'blk')), parts along dimension 0, may hold values from -6 to 6
- counts: int32 [768, 4], P(('band', 'blk')), parts along dimension 0, may hold values from 0 to 12
Outputs:
- correlograms: bfloat16 [768, 16, 1024], P(('band', 'blk')), parts along dimension 0
The draws below stay inside these ranges and needn't reach their ends.
There are 2 independent parts, one for each index of `band`. The reference program is written for one: setup_inputs(seed, part) draws one part's arguments, and reference() takes and returns one part's arrays. A program takes and returns all parts, laid end to end along the dimension named above; each array names one. Nothing has to cross between parts.
All inputs are finite; a program needn't handle non-finite values.
Results may differ from the reference program's by a relative error of at most 0.0085.
Values may be sent and summed in bfloat16 or wider, within the bound.
A program may use at most 64 MiB of HBM per device.

```python
import math
import jax
import jax.numpy as jnp
from jax import lax

STA_DEV = 24
SEG = 4
LAG = 1024
WINS = 12
NF = 512
STATIONS = 384
N_BLK = 16


def touch_ends(array, key, smallest, top_value):
    index_at = [jax.random.randint(jax.random.fold_in(key, axis), (), 0, length) for axis, length in enumerate(array.shape)]
    main_axis = array.shape.index(max(array.shape))
    next_to = index_at[:main_axis] + [(index_at[main_axis] + 1) % array.shape[main_axis]] + index_at[main_axis + 1:]
    return array.at[tuple(index_at)].set(smallest).at[tuple(next_to)].set(top_value)


def block_levels(rng, extent, shards, least, top_value):
    def one(dim, shards_of):
        steps = jax.random.uniform(jax.random.fold_in(jax.random.fold_in(rng, 6), dim), (shards_of,), jnp.float32, least / len(shards), top_value / len(shards))
        return jnp.repeat(jnp.exp(steps), extent[dim] // shards_of).reshape((-1,) + (1,) * (len(extent) - dim - 1))

    loudness = one(*shards[0])
    for cut in shards[1:]:
        loudness = loudness * one(*cut)
    return loudness


def scatter_about(stream_key, dims, deviation, limit, pieces=(), held_as=jnp.bfloat16):
    values = jax.random.normal(stream_key, dims, jnp.float32) * deviation
    if len(pieces) > 0:
        values = block_levels(stream_key, dims, pieces, -0.22, 0.18) * values
    return jnp.clip(values, min=-limit, max=limit).astype(held_as)


def setup_inputs(seed: int = 0, part: int = 0) -> dict:
    key_list = jax.random.split(jax.random.key(seed), 3)
    own_keys = jax.random.split(jax.random.fold_in(key_list[2], part), 3)
    spectra = scatter_about(own_keys[0], (STATIONS, SEG, 2 * NF), 1.0, 6.0, ((0, 16),))
    counts = touch_ends(jax.random.randint(own_keys[1], (STATIONS, SEG), 0, WINS + 1), jax.random.fold_in(own_keys[1], 1), 0, WINS).astype(jnp.int32)
    return dict(spectra=spectra, counts=counts)


def lag_table():
    bins = jnp.arange(LAG // 2, dtype=jnp.int32)
    taps = jnp.arange(LAG, dtype=jnp.int32) - LAG // 2
    phase = bins[:, None] * taps[None, :] % LAG
    angle = phase.astype(jnp.float32) * (2.0 * math.pi / LAG)
    return jnp.concatenate([jnp.cos(angle), jnp.sin(angle)], 0).astype(jnp.bfloat16)

def split_parts(block, block_counts):
    half = block.shape[2] // 2
    real_part = block[:, :, :half].astype(jnp.float32)
    imag_part = block[:, :, half:].astype(jnp.float32)
    inverse = lax.rsqrt(real_part * real_part + imag_part * imag_part + 0.25)
    return (real_part, imag_part, real_part * inverse, imag_part * inverse, block_counts.astype(jnp.float32))

def pair_beams(own, own_counts, other, other_counts):
    ra, ia, pa, qa, ca = split_parts(own, own_counts)
    rb, ib, pb, qb, cb = split_parts(other, other_counts)
    acc_re = 0.0
    acc_im = 0.0
    coh_re = 0.0
    coh_im = 0.0
    weight_sum = 0.0
    for seg in range(ra.shape[1]):
        weight = jnp.minimum(ca[:, None, seg], cb[None, :, seg])[:, :, None]
        xa_re = ra[:, None, seg, :]
        xa_im = ia[:, None, seg, :]
        xb_re = rb[None, :, seg, :]
        xb_im = ib[None, :, seg, :]
        acc_re = acc_re + weight * (xa_re * xb_re + xa_im * xb_im)
        acc_im = acc_im + weight * (xa_im * xb_re - xa_re * xb_im)
        ya_re = pa[:, None, seg, :]
        ya_im = qa[:, None, seg, :]
        yb_re = pb[None, :, seg, :]
        yb_im = qb[None, :, seg, :]
        coh_re = coh_re + weight * (ya_re * yb_re + ya_im * yb_im)
        coh_im = coh_im + weight * (ya_im * yb_re - ya_re * yb_im)
        weight_sum = weight_sum + weight
    total = jnp.maximum(weight_sum, 1.0)
    factor = (coh_re * coh_re + coh_im * coh_im) / (total * total * total)
    stack_re = acc_re * factor
    stack_im = acc_im * factor
    forward = jnp.concatenate([lax.optimization_barrier(jnp.sum(stack_re, 1)), lax.optimization_barrier(jnp.sum(stack_im, 1))], -1)
    backward = jnp.concatenate([lax.optimization_barrier(jnp.sum(stack_re, 0)), -lax.optimization_barrier(jnp.sum(stack_im, 0))], -1)
    return (forward, backward)

def reference(spectra, counts):
    table = lag_table()
    blocks = spectra.reshape(N_BLK, STA_DEV, SEG, spectra.shape[2])
    block_counts = counts.reshape(N_BLK, STA_DEV, SEG)

    def per_source(source):

        def per_offset(offset):
            target = (source + offset) % N_BLK
            forward, unused = pair_beams(blocks[source], block_counts[source], blocks[target], block_counts[target])
            return forward.astype(jnp.bfloat16)
        beam = lax.map(per_offset, jnp.arange(N_BLK, dtype=jnp.int32))
        traces = jnp.dot(beam.reshape(-1, beam.shape[2]), table, preferred_element_type=jnp.float32).astype(jnp.bfloat16)
        values = traces.astype(jnp.float32).reshape(N_BLK, STA_DEV, LAG)
        scale = jnp.sqrt(lax.optimization_barrier(jnp.mean(values * values, -1, keepdims=True)) + 1e-06)
        return jnp.transpose((values / scale).astype(jnp.bfloat16), (1, 0, 2))
    result = lax.map(per_source, jnp.arange(N_BLK, dtype=jnp.int32))
    return result.reshape(N_BLK * STA_DEV, N_BLK, LAG)
```

```python
import functools
import math

import jax
import jax.numpy as jnp
from jax import lax
from jax.experimental import pallas as pl
from jax.experimental.pallas import tpu as pltpu
from jax.sharding import PartitionSpec as P

LAG = 1024
LANES = 128
ROWS = 8
LEVELS = 12
BINS = 64
ZROWS = 136
XROWS = 72
F32 = jnp.float32
BF16 = jnp.bfloat16


def chip_of(place, chips, snake):
    if not snake:
        return place
    return jnp.where(place < chips // 2, 2 * place, 2 * (chips - 1 - place) + 1)


def place_of(chip, chips, snake):
    if not snake:
        return chip
    return jnp.where(chip % 2 == 0, chip // 2, chips - 1 - chip // 2)


def when(pred, fn):
    if isinstance(pred, bool):
        if pred:
            fn()
    else:
        pl.when(pred)(fn)


def lane_ids(rows):
    return lax.broadcasted_iota(jnp.int32, (rows, LANES), 1)


def row_ids(rows, lanes=LANES):
    return lax.broadcasted_iota(jnp.int32, (rows, lanes), 0)


def cos_sin(bins, rows):
    taps = lax.broadcasted_iota(jnp.int32, (rows, LAG), 1) - LAG // 2
    phase = (bins * taps) & (LAG - 1)
    quad = ((phase + LAG // 8) >> 8) & 3
    x = (((phase + LAG // 8) & (LAG // 4 - 1)) - LAG // 8).astype(F32) * (2.0 * math.pi / LAG)
    x2 = x * x
    sin = x * (1.0 + x2 * (-1.0 / 6 + x2 * (1.0 / 120 - x2 * (1.0 / 5040))))
    cos = 1.0 + x2 * (-0.5 + x2 * (1.0 / 24 + x2 * (-1.0 / 720 + x2 * (1.0 / 40320))))
    swap = (quad & 1) == 1
    a = jnp.where(swap, sin, cos)
    b = jnp.where(swap, cos, sin)
    a = jnp.where((quad == 1) | (quad == 2), -a, a)
    b = jnp.where(quad >= 2, -b, b)
    return a, b


def pair_kernel(
    n, snake, spec_ref, count_ref, beam_ref, table_ref,
    gathered, out_half, in_half, x_rows, p_rows, own_x, own_p, level_own, level_all,
    cube, stacked, beam_out, c_low, s_low, c_high, s_high, count_pad,
    l_send, l_recv, r_send, r_recv, h_send, h_recv, b_send, b_recv,
):
    segs, stations, spread = spec_ref.shape
    half = spread // 2
    chunks = half // 2 // BINS
    tiles = stations // ROWS
    both = 2 * stations
    chips = n // 2
    far = chips // 2
    groups = chips // 8
    size = segs * both
    mid = size // 2
    band = lax.axis_index("band")
    me = lax.axis_index("blk")
    core = me % 2
    chip = me // 2
    place = place_of(chip, chips, snake)
    left = chip_of((place + chips - 1) % chips, chips, snake) * 2 + core
    right = chip_of((place + 1) % chips, chips, snake) * 2 + core
    sibling = chip * 2 + 1 - core

    barrier = pltpu.get_barrier_semaphore()
    for other in (left, right, sibling):
        pl.semaphore_signal(
            barrier, inc=1, device_id=(band, other), device_id_type=pl.DeviceIdType.MESH
        )

    def remote(src, dst, send, recv, other):
        return pltpu.make_async_remote_copy(
            src_ref=src, dst_ref=dst, send_sem=send, recv_sem=recv,
            device_id=(band, other), device_id_type=pl.DeviceIdType.MESH,
        )

    def swap_copy(c):
        rows = 128 if c == 0 else segs * stations
        return remote(
            out_half.at[c, pl.ds(0, rows)], in_half.at[c, pl.ds(0, rows)],
            h_send.at[c], h_recv.at[c], sibling,
        )

    def ring(c, hop, first, last):
        full = size + both if first else size
        la, lb = (0, mid) if last else (0, full)
        ra, rb = (mid, full) if last else (0, full)
        a = remote(
            gathered.at[c, hop - 1, pl.ds(la, lb - la)], gathered.at[c, hop, pl.ds(la, lb - la)],
            l_send.at[c, hop - 1], l_recv.at[c, hop - 1], left,
        )
        back = (chips - hop + 1) % chips
        b = remote(
            gathered.at[c, back, pl.ds(ra, rb - ra)], gathered.at[c, chips - hop, pl.ds(ra, rb - ra)],
            r_send.at[c, hop - 1], r_recv.at[c, hop - 1], right,
        )
        return a, b

    def ring_do(c, hop, first, what):
        def go(last):
            def fn():
                for copy in ring(c, hop, first, last):
                    getattr(copy, what)()
            return fn
        when(hop < far, go(False))
        when(hop == far, go(True))

    def ring_start(c, hop, first=False):
        ring_do(c, hop, first, "start")

    def advance(c, hop, first=False):
        ring_do(c, hop, first, "wait_recv")
        when(hop < far, lambda: ring_start(c, hop + 1, first))

    lane24 = lane_ids(stations)
    low24 = lane24 < 64

    def piece(s, c, which):
        at = pl.multiple_of(which * (half // 2) + (c // 2) * LANES, LANES)
        re = spec_ref[s, :, pl.ds(at, LANES)].astype(F32)
        im = spec_ref[s, :, pl.ds(half + at, LANES)].astype(F32)
        if c % 2 == 0:
            return jnp.where(low24, re, pltpu.roll(im, 64, 1))
        return jnp.where(low24, pltpu.roll(re, 64, 1), im)

    count_pad[...] = jnp.zeros_like(count_pad)
    count_pad[0:segs, 0:stations] = count_ref[...].astype(F32)
    counted = count_pad[...].T
    seg24 = (lane24 & 7) >> 1
    plane = jnp.zeros((stations, LANES), F32)
    for s in range(segs):
        plane = jnp.where(seg24 == s, counted[:stations, s : s + 1], plane)

    for c in range(chunks):
        for s in range(segs):
            out_half[c, s * stations : (s + 1) * stations, :] = piece(s, c, 1 - core).astype(BF16)
        if c == 0:
            pad = jnp.zeros((128 - segs * stations - stations, LANES), F32)
            out_half[0, segs * stations : 128, :] = jnp.concatenate([plane, pad], 0).astype(BF16)
            pl.semaphore_wait(barrier, 3)
        swap_copy(c).start()

    first_core = core == 0

    def mixed(mine, theirs):
        rows = []
        for t in range(tiles):
            a = mine[t * ROWS : (t + 1) * ROWS]
            b = theirs[t * ROWS : (t + 1) * ROWS]
            rows += [jnp.where(first_core, a, b), jnp.where(first_core, b, a)]
        return jnp.concatenate(rows, 0).astype(BF16)

    def assemble(c):
        swap_copy(c).wait_recv()
        for s in range(segs):
            theirs = in_half[c, s * stations : (s + 1) * stations, :].astype(F32)
            gathered[c, 0, s * both : (s + 1) * both, :] = mixed(piece(s, c, core), theirs)
        if c == 0:
            theirs = in_half[0, segs * stations : 128, :].astype(F32)[:stations]
            gathered[0, 0, size : size + both, :] = mixed(plane, theirs)

    assemble(0)
    ring_start(0, 1, True)

    for c in range(1, chunks):
        assemble(c)

    low = row_ids(16, LAG)
    c_low[...], s_low[...] = cos_sin(low, 16)
    high = row_ids(half // 16, LAG) * 16
    c_high[...], s_high[...] = cos_sin(high, half // 16)

    def table_rows(h):
        a = c_high[pl.ds(h, 1), :]
        b = s_high[pl.ds(h, 1), :]
        at = (h // 4) * 128 + (h % 4) * 16
        table_ref[pl.ds(pl.multiple_of(at, 16), 16), :] = (
            a * c_low[...] - b * s_low[...]
        ).astype(BF16)
        table_ref[pl.ds(pl.multiple_of(at + 64, 16), 16), :] = (
            b * c_low[...] + a * s_low[...]
        ).astype(BF16)

    parts = half // 16 // 4

    def table_part(x):
        def step(h, carry):
            table_rows(x * parts + h)
            return carry
        lax.fori_loop(0, parts, step, 0)

    lane8 = lane_ids(ROWS)
    lane48 = lane_ids(both)

    def masks_own():
        own = gathered[0, 0, size : size + both, :].astype(F32)
        level_own[...] = jnp.where(own >= ((lane48 >> 3) + 1).astype(F32), 1.0, 0.0)

    def begin():
        for x in range(far):
            table_part(x) if x < 4 else None
            hop = x + 1
            advance(0, hop, True)
            if hop == far // 2:
                ring_start(1, 1)
            if hop > far // 2:
                advance(1, hop - far // 2)
        if chunks > 2:
            ring_start(2, 1)

    begin()
    masks_own()

    row128 = row_ids(LANES)
    own_count = gathered[0, 0, size : size + both, :].astype(F32)
    for e in range(groups):
        for t in range(tiles):
            stack = jnp.concatenate(
                [gathered[0, e * 8 + d, size + t * 16 : size + t * 16 + 16, :] for d in range(8)], 0
            )
            turned = stack.astype(F32).T
            level_all[e, :, t * LANES : (t + 1) * LANES] = jnp.where(
                turned >= ((row128 >> 3) + 1).astype(F32), 1.0, 0.0
            )[: LEVELS * 8].astype(BF16)
            total = jnp.zeros((both, LANES), F32)
            for s in range(segs):
                total = total + jnp.minimum(own_count[:, 2 * s : 2 * s + 1], turned[2 * s : 2 * s + 1, :])
            total = jnp.maximum(total, 1.0)
            share = 1.0 / total
            cube[e, :, t * LANES : (t + 1) * LANES] = share * share * share

    def prepare_own(c):
        xs, ps = [], []
        for s in range(segs):
            x = gathered[c, 0, s * both : (s + 1) * both, :].astype(F32)
            sq = x * x
            xs.append(x)
            ps.append(x * lax.rsqrt(sq + pltpu.roll(sq, 64, 1) + 0.25))
        seg8 = (lane8 & 7) >> 1
        part8 = lane8 & 1
        sign = (1 - 2 * part8).astype(F32)
        for g in range(BINS // 16):
            at_re = part8 * 64 + g * 16 + (lane8 >> 3)
            at_im = (1 - part8) * 64 + g * 16 + (lane8 >> 3)
            for values, target in ((xs, own_x), (ps, own_p)):
                for r in range(0, both, ROWS):
                    re = im = None
                    for s in range(segs):
                        v = values[s][r : r + ROWS]
                        a = jnp.take_along_axis(v, at_re, axis=1)
                        b = jnp.take_along_axis(v, at_im, axis=1)
                        re = a if s == 0 else jnp.where(seg8 == s, a, re)
                        im = b if s == 0 else jnp.where(seg8 == s, b, im)
                    target[g, r : r + ROWS, :] = re
                    target[g, both + r : both + r + ROWS, :] = im * sign

    def prepare_all(c, e):
        for s in range(segs):
            for t in range(tiles):
                stack = jnp.concatenate(
                    [gathered[c, e * 8 + d, s * both + t * 16 : s * both + t * 16 + 16, :] for d in range(8)], 0
                )
                turned = stack.astype(F32).T
                re, im = turned[:64], turned[64:]
                inv = lax.rsqrt(re * re + im * im + 0.25)
                x_rows[t, (2 * s) * XROWS : (2 * s) * XROWS + 64, :] = re
                x_rows[t, (2 * s + 1) * XROWS : (2 * s + 1) * XROWS + 64, :] = im
                p_rows[t, (2 * s) * XROWS : (2 * s) * XROWS + 64, :] = re * inv
                p_rows[t, (2 * s + 1) * XROWS : (2 * s + 1) * XROWS + 64, :] = im * inv

    depth = LEVELS * 8

    def sixteen(g, e):
        for f in range(16):
            index = (lane8 & 7) + 8 * f
            bin_at = g * 16 + f
            products = []
            for own, rows in ((own_x, x_rows), (own_p, p_rows)):
                pieces = []
                for r in range(0, 2 * both, ROWS):
                    m = r % both
                    v = jnp.take_along_axis(own[g, r : r + ROWS, :], index, axis=1)
                    pieces.append(v * level_own[m : m + ROWS, :])
                lhs = jnp.concatenate(pieces, 0).astype(BF16)[:, :depth]
                cols = []
                for t in range(tiles):
                    x8 = rows[t, pl.ds(bin_at, 8, stride=XROWS), :]
                    x16 = jnp.concatenate([x8, x8], 0).astype(BF16)
                    cols.append(jnp.concatenate(
                        [x16 * level_all[e, k : k + 16, t * LANES : (t + 1) * LANES] for k in range(0, depth, 16)], 0
                    ))
                rhs = jnp.concatenate(cols, 1)
                products.append(jnp.dot(lhs, rhs, preferred_element_type=F32))
            cross, coh = products
            hr, hi = coh[:both], coh[both:]
            factor = (hr * hr + hi * hi) * cube[e]
            re = cross[:both] * factor
            im = cross[both:] * factor
            re = sum(re[:, t * LANES : (t + 1) * LANES] for t in range(tiles))
            im = sum(im[:, t * LANES : (t + 1) * LANES] for t in range(tiles))
            stacked[pl.ds(bin_at, both, stride=ZROWS), :] = re
            stacked[pl.ds(64 + bin_at, both, stride=ZROWS), :] = im

    hops = far // 4

    def chunk(c, carry):
        prepare_own(c)

        def group(e, carry):
            prepare_all(c, e)

            def quarter(g, carry):
                sixteen(g, e)

                def move():
                    def one(x, carry):
                        r = g // 2

                        @pl.when(c + 1 < chunks)
                        def _():
                            advance(c + 1, far // 2 + r * hops + x + 1)

                        @pl.when(c + 2 < chunks)
                        def _():
                            advance(c + 2, r * hops + x + 1)
                        return carry
                    lax.fori_loop(0, hops, one, 0)

                    @pl.when((g == 3) & (c + 3 < chunks))
                    def _():
                        ring_start(c + 3, 1)

                pl.when((g % 2 == 1) & (e == 0))(move)
                return carry

            lax.fori_loop(0, BINS // 16, quarter, 0)

            for o in range(2):
                q = core if o == 0 else 1 - core
                mine = 2 * chip + q
                lane = lane_ids(n)
                where = place + e * 8 + (lane >> 4)
                where = jnp.where(where >= chips, where - chips, where)
                k = 2 * chip_of(where, chips, snake) + ((lane >> 3) & 1) - mine
                k = jnp.where(k < 0, k + n, k)
                pick = jnp.where(k == row_ids(n), 1.0, 0.0).astype(BF16)

                def station(i, carry):
                    row = ((i >> 3) * 16 + q * 8 + (i & 7)) * ZROWS
                    z = stacked[pl.ds(pl.multiple_of(row, 8), LANES), :].astype(BF16)
                    beam = lax.dot_general(
                        pick, z, (((1,), (1,)), ((), ())), preferred_element_type=F32
                    )
                    at = pl.ds(pl.multiple_of(i * n, 16), n)
                    if groups > 1:
                        old = beam_ref[core, c, at, :] if o == 0 else beam_out[c, at, :]
                        beam = beam + jnp.where(e > 0, old.astype(F32), 0.0)
                    if o == 0:
                        beam_ref[core, c, at, :] = beam.astype(BF16)
                    else:
                        beam_out[c, at, :] = beam.astype(BF16)
                    return carry

                lax.fori_loop(0, stations, station, 0, unroll=8)
            return carry

        if groups == 1:
            group(0, 0)
        else:
            lax.fori_loop(0, groups, group, 0)
        beam_copy(c).start()
        return carry

    def beam_copy(c):
        return remote(beam_out.at[c], beam_ref.at[core, c], b_send.at[c], b_recv.at[c], sibling)

    lax.fori_loop(0, chunks, chunk, 0)

    for c in range(chunks):
        swap_copy(c).wait_send()

    def drain(c, first):
        def one(hop, carry):
            ring_do(c, hop, first, "wait_send")
            return carry
        lax.fori_loop(1, far + 1, one, 0)

    drain(0, True)

    def rest(c, carry):
        drain(c, False)
        return carry

    lax.fori_loop(1, chunks, rest, 0)
    for c in range(chunks):
        beam_copy(c).wait_send()
        remote(
            beam_out.at[c], beam_ref.at[1 - core, c], b_send.at[c], b_recv.at[c], sibling
        ).wait_recv()


def pair_beams(spectra, counts, n, snake):
    segs, stations, spread = spectra.shape
    half = spread // 2
    chunks = half // 2 // BINS
    chips = n // 2
    far = chips // 2
    groups = chips // 8
    tiles = stations // ROWS
    both = 2 * stations
    dma = pltpu.SemaphoreType.DMA
    pairs = n * stations * stations * half
    return pl.pallas_call(
        functools.partial(pair_kernel, n, snake),
        out_shape=(
            jax.ShapeDtypeStruct((2, chunks, stations * n, LANES), BF16),
            jax.ShapeDtypeStruct((spread, LAG), BF16),
        ),
        in_specs=[pl.BlockSpec(memory_space=pltpu.VMEM)] * 2,
        out_specs=[pl.BlockSpec(memory_space=pltpu.VMEM)] * 2,
        scratch_shapes=[
            pltpu.VMEM((chunks, chips, segs * both + both, LANES), BF16),
            pltpu.VMEM((chunks, 128, LANES), BF16),
            pltpu.VMEM((chunks, 128, LANES), BF16),
            pltpu.VMEM((tiles, 8 * XROWS, LANES), F32),
            pltpu.VMEM((tiles, 8 * XROWS, LANES), F32),
            pltpu.VMEM((BINS // 16, 2 * both, LANES), F32),
            pltpu.VMEM((BINS // 16, 2 * both, LANES), F32),
            pltpu.VMEM((both, LANES), F32),
            pltpu.VMEM((groups, LEVELS * 8, tiles * LANES), BF16),
            pltpu.VMEM((groups, both, tiles * LANES), F32),
            pltpu.VMEM((both * ZROWS, LANES), F32),
            pltpu.VMEM((chunks, stations * n, LANES), BF16),
            pltpu.VMEM((16, LAG), F32), pltpu.VMEM((16, LAG), F32),
            pltpu.VMEM((half // 16, LAG), F32), pltpu.VMEM((half // 16, LAG), F32),
            pltpu.VMEM((LANES, LANES), F32),
            dma((chunks, far)), dma((chunks, far)), dma((chunks, far)), dma((chunks, far)),
            dma((chunks,)), dma((chunks,)), dma((chunks,)), dma((chunks,)),
        ],
        compiler_params=pltpu.CompilerParams(
            collective_id=0, has_side_effects=True, vmem_limit_bytes=48 * 1024 * 1024
        ),
        cost_estimate=pl.CostEstimate(
            flops=66 * pairs, bytes_accessed=2 * spectra.size, transcendentals=0
        ),
        name="pair_beams",
    )(spectra, counts)


def lag_kernel(beam_ref, table_ref, out_ref):
    halves, chunks = beam_ref.shape[:2]
    rows = jnp.concatenate(
        [beam_ref[h, c] for h in range(halves) for c in range(chunks)], 1
    )
    trace = jnp.dot(rows, table_ref[...], preferred_element_type=F32)
    values = trace.astype(BF16).astype(F32)
    scale = jnp.sqrt(jnp.mean(values * values, -1, keepdims=True) + 1e-06)
    out_ref[...] = (values / scale).astype(BF16)


def lag_traces(beams, table):
    halves, chunks, rows, _ = beams.shape
    block = 128
    return pl.pallas_call(
        lag_kernel,
        grid=(rows // block,),
        out_shape=jax.ShapeDtypeStruct((rows, LAG), BF16),
        in_specs=[
            pl.BlockSpec((halves, chunks, block, LANES), lambda i: (0, 0, i, 0)),
            pl.BlockSpec(table.shape, lambda i: (0, 0)),
        ],
        out_specs=pl.BlockSpec((block, LAG), lambda i: (i, 0)),
        compiler_params=pltpu.CompilerParams(vmem_limit_bytes=32 * 1024 * 1024),
        name="lag_traces",
    )(beams, table)


def shards(snake, spectra, counts):
    n = lax.axis_size("blk")
    stations, segs, spread = spectra.shape
    beams, table = pair_beams(spectra.transpose(1, 0, 2), counts.T, n, snake)
    out = lag_traces(beams, table)
    return out.reshape(stations, n, LAG)


def solution(mesh):
    snake = mesh.shape["blk"] == 16
    return jax.shard_map(
        functools.partial(shards, snake),
        mesh=mesh,
        in_specs=(P(("band", "blk"), None, None), P(("band", "blk"), None)),
        out_specs=P(("band", "blk"), None, None),
        check_vma=False,
    )
```

```python
import functools
import math

import jax
import jax.numpy as jnp
from jax import lax
from jax.experimental import pallas as pl
from jax.experimental.pallas import tpu as pltpu
from jax.sharding import PartitionSpec as P

LAG = 1024
LANES = 128
ROWS = 8
LEVELS = 12
BINS = 64
ZROWS = 136
XROWS = 72
UNROLL = 32
F32 = jnp.float32
BF16 = jnp.bfloat16


def chip_of(place, chips, snake):
    if not snake:
        return place
    return jnp.where(place < chips // 2, 2 * place, 2 * (chips - 1 - place) + 1)


def place_of(chip, chips, snake):
    if not snake:
        return chip
    return jnp.where(chip % 2 == 0, chip // 2, chips - 1 - chip // 2)


def when(pred, fn):
    if isinstance(pred, bool):
        if pred:
            fn()
    else:
        pl.when(pred)(fn)


def lane_ids(rows):
    return lax.broadcasted_iota(jnp.int32, (rows, LANES), 1)


def row_ids(rows, lanes=LANES):
    return lax.broadcasted_iota(jnp.int32, (rows, lanes), 0)


def cos_sin(bins, rows):
    taps = lax.broadcasted_iota(jnp.int32, (rows, LAG), 1) - LAG // 2
    phase = (bins * taps) & (LAG - 1)
    quad = ((phase + LAG // 8) >> 8) & 3
    x = (((phase + LAG // 8) & (LAG // 4 - 1)) - LAG // 8).astype(F32) * (2.0 * math.pi / LAG)
    x2 = x * x
    sin = x * (1.0 + x2 * (-1.0 / 6 + x2 * (1.0 / 120 - x2 * (1.0 / 5040))))
    cos = 1.0 + x2 * (-0.5 + x2 * (1.0 / 24 + x2 * (-1.0 / 720 + x2 * (1.0 / 40320))))
    swap = (quad & 1) == 1
    a = jnp.where(swap, sin, cos)
    b = jnp.where(swap, cos, sin)
    a = jnp.where((quad == 1) | (quad == 2), -a, a)
    b = jnp.where(quad >= 2, -b, b)
    return a, b


def pair_kernel(
    n, snake, spec_ref, count_ref, beam_ref, table_ref,
    gathered, out_half, x_rows, p_rows, own_x, own_p, lhs_x, lhs_p, level_own, level_all,
    cube, stacked, picks, sums, beam_out, c_low, s_low, c_high, s_high, count_pad,
    l_send, l_recv, r_send, r_recv, h_send, h_recv, b_send, b_recv,
):
    segs, stations, spread = spec_ref.shape
    half = spread // 2
    chunks = half // 2 // BINS
    tiles = stations // ROWS
    both = 2 * stations
    chips = n // 2
    far = chips // 2
    groups = chips // 4
    size = segs * stations
    depth = LEVELS * 8
    band = lax.axis_index("band")
    me = lax.axis_index("blk")
    core = me % 2
    chip = me // 2
    place = place_of(chip, chips, snake)
    left = chip_of((place + chips - 1) % chips, chips, snake) * 2
    right = chip_of((place + 1) % chips, chips, snake) * 2
    sibling = chip * 2 + 1 - core

    barrier = pltpu.get_barrier_semaphore()
    for other in (left, left + 1, right, right + 1, sibling):
        pl.semaphore_signal(
            barrier, inc=1, device_id=(band, other), device_id_type=pl.DeviceIdType.MESH
        )

    def remote(src, dst, send, recv, other):
        return pltpu.make_async_remote_copy(
            src_ref=src, dst_ref=dst, send_sem=send, recv_sem=recv,
            device_id=(band, other), device_id_type=pl.DeviceIdType.MESH,
        )

    def rows_of(c):
        return pl.ds(0, 128 if c == 0 else size)

    def swap_copy(c, q):
        return remote(
            out_half.at[c, rows_of(c)], gathered.at[c, 0, q, rows_of(c)],
            h_send.at[c], h_recv.at[c], sibling,
        )

    def first_copies(c, q):
        same, cross = (gathered.at[c, 0, core, rows_of(c)], out_half.at[c, rows_of(c)])
        copies = []
        for other, slot, send, recv in (
            (left, 1, l_send, l_recv), (right, chips - 1, r_send, r_recv)
        ):
            for k, src in enumerate((same, cross)):
                which = core if k == 0 else 1 - core
                copies.append(remote(
                    src, gathered.at[c, slot, q, rows_of(c)],
                    send.at[c, 0, k], recv.at[c, 0, q], other + which,
                ))
        return copies

    def arrived_first(c):
        for slot, recv, send, other in (
            (1, l_recv, l_send, left), (chips - 1, r_recv, r_send, right)
        ):
            for q in range(2):
                remote(
                    out_half.at[c, rows_of(c)], gathered.at[c, slot, q, rows_of(c)],
                    send.at[c, 0, q], recv.at[c, 0, q], other,
                ).wait_recv()

    def ring(c, hop, last, first):
        rows = pl.ds(0, 128 if first else size)
        lq = pl.ds(0, 1) if last else pl.ds(0, 2)
        rq = pl.ds(1, 1) if last else pl.ds(0, 2)
        a = remote(
            gathered.at[c, hop - 1, lq, rows], gathered.at[c, hop, lq, rows],
            l_send.at[c, hop - 1, 0], l_recv.at[c, hop - 1, 0], left + core,
        )
        b = remote(
            gathered.at[c, chips - hop + 1, rq, rows], gathered.at[c, chips - hop, rq, rows],
            r_send.at[c, hop - 1, 0], r_recv.at[c, hop - 1, 0], right + core,
        )
        return a, b

    def ring_do(c, hop, what):
        def go(last, first):
            def fn():
                for copy in ring(c, hop, last, first):
                    getattr(copy, what)()
            return fn
        if isinstance(c, int) and isinstance(hop, int):
            go(hop == far, c == 0)()
            return
        for last in (False, True):
            for first in (False, True):
                right_hop = (hop == far) if last else (hop < far)
                right_part = (c == 0) if first else (c > 0)
                pl.when(right_hop & right_part)(go(last, first))

    def advance(c, hop):
        if isinstance(hop, int) and hop == 1:
            arrived_first(c)
        else:
            ring_do(c, hop, "wait_recv")
        when(hop < far, lambda: ring_do(c, hop + 1, "start"))

    lane24 = lane_ids(stations)
    low24 = lane24 < 64

    def piece(s, c, which):
        at = pl.multiple_of(which * (half // 2) + (c // 2) * LANES, LANES)
        re = spec_ref[s, :, pl.ds(at, LANES)].astype(F32)
        im = spec_ref[s, :, pl.ds(half + at, LANES)].astype(F32)
        if c % 2 == 0:
            return jnp.where(low24, re, pltpu.roll(im, 64, 1))
        return jnp.where(low24, pltpu.roll(re, 64, 1), im)

    count_pad[...] = jnp.zeros_like(count_pad)
    count_pad[0:segs, 0:stations] = count_ref[...].astype(F32)
    counted = count_pad[...].T
    seg24 = (lane24 & 7) >> 1
    plane = jnp.zeros((stations, LANES), F32)
    for s in range(segs):
        plane = jnp.where(seg24 == s, counted[:stations, s : s + 1], plane)
    pad = jnp.zeros((128 - size - stations, LANES), F32)

    for c in range(chunks):
        away = [piece(s, c, 1 - core) for s in range(segs)]
        home = [piece(s, c, core) for s in range(segs)]
        if c == 0:
            away += [plane, pad]
            home += [plane, pad]
        out_half[c, rows_of(c), :] = jnp.concatenate(away, 0).astype(BF16)
        gathered[c, 0, core, rows_of(c), :] = jnp.concatenate(home, 0).astype(BF16)
        if c == 0:
            pl.semaphore_wait(barrier, 5)
        swap_copy(c, core).start()
        for copy in first_copies(c, core):
            copy.start()

    low = row_ids(16, LAG)
    c_low[...], s_low[...] = cos_sin(low, 16)
    high = row_ids(half // 16, LAG) * 16
    c_high[...], s_high[...] = cos_sin(high, half // 16)

    def table_rows(h, carry):
        a = c_high[pl.ds(h, 1), :]
        b = s_high[pl.ds(h, 1), :]
        at = (h // 4) * 128 + (h % 4) * 16
        table_ref[pl.ds(pl.multiple_of(at, 16), 16), :] = (
            a * c_low[...] - b * s_low[...]
        ).astype(BF16)
        table_ref[pl.ds(pl.multiple_of(at + 64, 16), 16), :] = (
            b * c_low[...] + a * s_low[...]
        ).astype(BF16)
        return carry

    lax.fori_loop(0, half // 16, table_rows, 0, unroll=2)

    def sum_picks(e, carry):
        lane = lax.broadcasted_iota(jnp.int32, (LANES, ROWS * n), 0)
        col = lax.broadcasted_iota(jnp.int32, (LANES, ROWS * n), 1)
        d = (lane >> 4) & 3
        off = jnp.where(
            d == 0, (chips - 2 * e) % chips,
            jnp.where(d == 1, 2 * e + 1, jnp.where(d == 2, chips - 2 * e - 1, 2 * e + 2)),
        )
        where = place + off
        where = jnp.where(where >= chips, where - chips, where)
        block = 2 * chip_of(where, chips, snake) + ((lane >> 3) & 1)
        for q in range(2):
            k = block - (2 * chip + q)
            k = jnp.where(k < 0, k + n, k)
            for u in range(ROWS):
                picks[e, q, u * LANES : (u + 1) * LANES, :] = jnp.where(
                    col == u * n + k, 1.0, 0.0
                ).astype(BF16)
        return carry

    lax.fori_loop(0, groups, sum_picks, 0)
    sums[...] = jnp.zeros_like(sums)

    lane8 = lane_ids(ROWS)
    lane48 = lane_ids(both)
    row128 = row_ids(LANES)

    def wait_swap(c):
        remote(
            out_half.at[c, rows_of(c)], gathered.at[c, 0, 1 - core, rows_of(c)],
            h_send.at[c], h_recv.at[c], sibling,
        ).wait_recv()

    def eight(c, slot, q, row):
        base = row // 16 * 16
        return gathered[c, slot, q, pl.ds(base, 16), :].astype(F32)[row - base : row - base + 8]

    def own_rows(c, start):
        return jnp.concatenate(
            [eight(c, 0, q, start + t * ROWS) for t in range(tiles) for q in range(2)], 0
        )

    for c in range(chunks):
        wait_swap(c)
    own_count = own_rows(0, size)
    level_own[...] = jnp.where(own_count >= ((lane48 >> 3) + 1).astype(F32), 1.0, 0.0)

    def prepare_own(c):
        planes = [own_rows(c, s * stations) for s in range(segs)]
        seg8 = (lane8 & 7) >> 1
        part8 = lane8 & 1
        sign = (1 - 2 * part8).astype(F32)
        swap = lane8 ^ 1
        for g in range(BINS // 16):
            at = part8 * 64 + g * 16 + (lane8 >> 3)
            for r in range(0, both, ROWS):
                re = None
                for s in range(segs):
                    v = jnp.take_along_axis(planes[s][r : r + ROWS], at, axis=1)
                    re = v if s == 0 else jnp.where(seg8 == s, v, re)
                im = jnp.take_along_axis(re, swap, axis=1) * sign
                inv = lax.rsqrt(re * re + im * im + 0.25)
                own_x[g, r : r + ROWS, :] = re
                own_x[g, both + r : both + r + ROWS, :] = im
                own_p[g, r : r + ROWS, :] = re * inv
                own_p[g, both + r : both + r + ROWS, :] = im * inv

        def spread_one(g, carry):
            for f in range(16):
                index = (lane8 & 7) + 8 * f
                for own, lhs in ((own_x, lhs_x), (own_p, lhs_p)):
                    for r in range(0, 2 * both, 16):
                        rows = []
                        for o in (r, r + ROWS):
                            m = o % both
                            v = jnp.take_along_axis(own[g, o : o + ROWS, :], index, axis=1)
                            rows.append(v * level_own[m : m + ROWS, :])
                        lhs[c, g * 16 + f, r : r + 16, :] = jnp.concatenate(rows, 0).astype(BF16)
            return carry

        lax.fori_loop(0, BINS // 16, spread_one, 0)

    def slots_of(e):
        return ((chips - 2 * e) % chips, 2 * e + 1, chips - 2 * e - 1, 2 * e + 2)

    def stack(c, e, start, part):
        slots = slots_of(e)
        rows = [
            eight(c, slots[d], q, start + t * ROWS)
            for t in ((0, 1) if part == 0 else (2,)) for d in range(4) for q in range(2)
        ]
        if part == 1:
            rows.append(jnp.zeros((64, LANES), F32))
        return jnp.concatenate(rows, 0).T

    def prepare_group(e):
        for v in range(2):
            turned = stack(0, e, size, v)
            level_all[:, v * LANES : (v + 1) * LANES] = jnp.where(
                turned >= ((row128 >> 3) + 1).astype(F32), 1.0, 0.0
            )[:depth].astype(BF16)
            total = jnp.zeros((both, LANES), F32)
            mine = own_rows(0, size)
            for s in range(segs):
                total = total + jnp.minimum(mine[:, 2 * s : 2 * s + 1], turned[2 * s : 2 * s + 1, :])
            total = jnp.maximum(total, 1.0)
            share = 1.0 / total
            cube[:, v * LANES : (v + 1) * LANES] = share * share * share

    def prepare_all(c, e):
        for s in range(segs):
            for v in range(2):
                turned = stack(c, e, s * stations, v)
                re, im = turned[:64], turned[64:]
                inv = lax.rsqrt(re * re + im * im + 0.25)
                x_rows[v, (2 * s) * XROWS : (2 * s) * XROWS + 64, :] = re
                x_rows[v, (2 * s + 1) * XROWS : (2 * s + 1) * XROWS + 64, :] = im
                p_rows[v, (2 * s) * XROWS : (2 * s) * XROWS + 64, :] = re * inv
                p_rows[v, (2 * s + 1) * XROWS : (2 * s + 1) * XROWS + 64, :] = im * inv

    def one_bin(c, at):
        products = []
        for lhs, rows in ((lhs_x, x_rows), (lhs_p, p_rows)):
            cols = []
            for v in range(2):
                x8 = rows[v, pl.ds(at, 8, stride=XROWS), :]
                x16 = jnp.concatenate([x8, x8], 0).astype(BF16)
                cols.append(jnp.concatenate(
                    [x16 * level_all[k : k + 16, v * LANES : (v + 1) * LANES] for k in range(0, depth, 16)], 0
                ))
            products.append(jnp.dot(
                lhs[c, at, :, :depth], jnp.concatenate(cols, 1), preferred_element_type=F32
            ))
        cross, coh = products
        hr, hi = coh[:both], coh[both:]
        factor = (hr * hr + hi * hi) * cube[...]
        re = cross[:both] * factor
        im = cross[both:] * factor
        stacked[pl.ds(at, both, stride=ZROWS), :] = re[:, :LANES] + re[:, LANES:]
        stacked[pl.ds(64 + at, both, stride=ZROWS), :] = im[:, :LANES] + im[:, LANES:]

    def beam_copy(c, h):
        return remote(beam_out.at[c], beam_ref.at[h, c], b_send.at[c], b_recv.at[c], sibling)

    def reduce_beams(c, e):
        for o in range(2):
            q = core if o == 0 else 1 - core
            for t in range(tiles):
                base = (t * 16 + q * 8) * ZROWS
                z = jnp.concatenate([
                    stacked[pl.ds(pl.multiple_of(base + u * ZROWS, 8), LANES), :].astype(BF16)
                    for u in range(ROWS)
                ], 1)
                part = jnp.dot(z, picks[e, q], preferred_element_type=F32)
                sums[c, o, t] = sums[c, o, t] + part

        @pl.when(e == groups - 1)
        def _():
            for o in range(2):
                for t in range(tiles):
                    rows = sums[c, o, t].T.astype(BF16)
                    at = pl.ds(t * ROWS * n, ROWS * n)
                    if o == 0:
                        beam_ref[core, c, at, :] = rows
                    else:
                        beam_out[c, at, :] = rows
            beam_copy(c, core).start()

    for c in range(chunks):
        prepare_own(c)
        if c > 0:
            advance(c - 1, 1)
    advance(chunks - 1, 1)
    advance(0, 2)

    def work(step, carry):
        e = step // chunks
        c = step % chunks

        @pl.when(c == 0)
        def _():
            prepare_group(e)

        prepare_all(c, e)

        def bins(x, carry):
            for f in range(UNROLL):
                one_bin(c, x * UNROLL + f)
            index = chunks + 1 + 2 * step + x

            @pl.when(index < far * chunks)
            def _():
                advance(index % chunks, index // chunks + 1)
            return carry

        lax.fori_loop(0, BINS // UNROLL, bins, 0)
        reduce_beams(c, e)
        return carry

    lax.fori_loop(0, groups * chunks, work, 0)

    for c in range(chunks):
        swap_copy(c, core).wait_send()
        for copy in first_copies(c, core):
            copy.wait_send()

    def drain(index, carry):
        ring_do(index % chunks, index // chunks + 2, "wait_send")
        return carry

    lax.fori_loop(0, (far - 1) * chunks, drain, 0)
    for c in range(chunks):
        beam_copy(c, core).wait_send()
        beam_copy(c, 1 - core).wait_recv()


def pair_beams(spectra, counts, n, snake):
    segs, stations, spread = spectra.shape
    half = spread // 2
    chunks = half // 2 // BINS
    chips = n // 2
    far = chips // 2
    groups = chips // 4
    tiles = stations // ROWS
    both = 2 * stations
    dma = pltpu.SemaphoreType.DMA
    pairs = n * stations * stations * half
    return pl.pallas_call(
        functools.partial(pair_kernel, n, snake),
        out_shape=(
            jax.ShapeDtypeStruct((2, chunks, stations * n, LANES), BF16),
            jax.ShapeDtypeStruct((spread, LAG), BF16),
        ),
        in_specs=[pl.BlockSpec(memory_space=pltpu.VMEM)] * 2,
        out_specs=[pl.BlockSpec(memory_space=pltpu.VMEM)] * 2,
        scratch_shapes=[
            pltpu.VMEM((chunks, chips, 2, 128, LANES), BF16),
            pltpu.VMEM((chunks, 128, LANES), BF16),
            pltpu.VMEM((2, 8 * XROWS, LANES), F32),
            pltpu.VMEM((2, 8 * XROWS, LANES), F32),
            pltpu.VMEM((BINS // 16, 2 * both, LANES), F32),
            pltpu.VMEM((BINS // 16, 2 * both, LANES), F32),
            pltpu.VMEM((chunks, BINS, 2 * both, LANES), BF16),
            pltpu.VMEM((chunks, BINS, 2 * both, LANES), BF16),
            pltpu.VMEM((both, LANES), F32),
            pltpu.VMEM((LEVELS * 8, 2 * LANES), BF16),
            pltpu.VMEM((both, 2 * LANES), F32),
            pltpu.VMEM((both * ZROWS, LANES), F32),
            pltpu.VMEM((groups, 2, ROWS * LANES, ROWS * n), BF16),
            pltpu.VMEM((chunks, 2, tiles, LANES, ROWS * n), F32),
            pltpu.VMEM((chunks, stations * n, LANES), BF16),
            pltpu.VMEM((16, LAG), F32), pltpu.VMEM((16, LAG), F32),
            pltpu.VMEM((half // 16, LAG), F32), pltpu.VMEM((half // 16, LAG), F32),
            pltpu.VMEM((LANES, LANES), F32),
            dma((chunks, far, 2)), dma((chunks, far, 2)), dma((chunks, far, 2)), dma((chunks, far, 2)),
            dma((chunks,)), dma((chunks,)), dma((chunks,)), dma((chunks,)),
        ],
        compiler_params=pltpu.CompilerParams(
            collective_id=0, has_side_effects=True, vmem_limit_bytes=60 * 1024 * 1024
        ),
        cost_estimate=pl.CostEstimate(
            flops=66 * pairs, bytes_accessed=2 * spectra.size, transcendentals=0
        ),
        name="pair_beams",
    )(spectra, counts)


def lag_kernel(beam_ref, table_ref, out_ref):
    halves, chunks = beam_ref.shape[:2]
    rows = jnp.concatenate(
        [beam_ref[h, c] for h in range(halves) for c in range(chunks)], 1
    )
    trace = jnp.dot(rows, table_ref[...], preferred_element_type=F32)
    values = trace.astype(BF16).astype(F32)
    scale = jnp.sqrt(jnp.mean(values * values, -1, keepdims=True) + 1e-06)
    out_ref[...] = (values / scale).astype(BF16)


def lag_traces(beams, table):
    halves, chunks, rows, _ = beams.shape
    block = 128
    return pl.pallas_call(
        lag_kernel,
        grid=(rows // block,),
        out_shape=jax.ShapeDtypeStruct((rows, LAG), BF16),
        in_specs=[
            pl.BlockSpec((halves, chunks, block, LANES), lambda i: (0, 0, i, 0)),
            pl.BlockSpec(table.shape, lambda i: (0, 0)),
        ],
        out_specs=pl.BlockSpec((block, LAG), lambda i: (i, 0)),
        compiler_params=pltpu.CompilerParams(vmem_limit_bytes=32 * 1024 * 1024),
        name="lag_traces",
    )(beams, table)


def shards(snake, spectra, counts):
    n = lax.axis_size("blk")
    stations, segs, spread = spectra.shape
    beams, table = pair_beams(spectra.transpose(1, 0, 2), counts.T, n, snake)
    out = lag_traces(beams, table)
    return out.reshape(stations, n, LAG)


def solution(mesh):
    snake = mesh.shape["blk"] == 16
    return jax.shard_map(
        functools.partial(shards, snake),
        mesh=mesh,
        in_specs=(P(("band", "blk"), None, None), P(("band", "blk"), None)),
        out_specs=P(("band", "blk"), None, None),
        check_vma=False,
    )
```

```python
import functools
import math

import jax
import jax.numpy as jnp
from jax import lax
from jax.experimental import pallas as pl
from jax.experimental.pallas import tpu as pltpu
from jax.sharding import PartitionSpec as P

LAG = 1024
LANES = 128
ROWS = 8
LEVELS = 12
BINS = 64
ZROWS = 72
XROWS = 72
PAIRS = BINS // 2
F32 = jnp.float32
BF16 = jnp.bfloat16


def chip_of(place, chips, snake):
    if not snake:
        return place
    return jnp.where(place < chips // 2, 2 * place, 2 * (chips - 1 - place) + 1)


def place_of(chip, chips, snake):
    if not snake:
        return chip
    return jnp.where(chip % 2 == 0, chip // 2, chips - 1 - chip // 2)


def when(pred, fn):
    if isinstance(pred, bool):
        if pred:
            fn()
    else:
        pl.when(pred)(fn)


def lane_ids(rows):
    return lax.broadcasted_iota(jnp.int32, (rows, LANES), 1)


def row_ids(rows, lanes=LANES):
    return lax.broadcasted_iota(jnp.int32, (rows, lanes), 0)


def cos_sin(bins, rows):
    taps = lax.broadcasted_iota(jnp.int32, (rows, LAG), 1) - LAG // 2
    phase = (bins * taps) & (LAG - 1)
    quad = ((phase + LAG // 8) >> 8) & 3
    x = (((phase + LAG // 8) & (LAG // 4 - 1)) - LAG // 8).astype(F32) * (2.0 * math.pi / LAG)
    x2 = x * x
    sin = x * (1.0 + x2 * (-1.0 / 6 + x2 * (1.0 / 120 - x2 * (1.0 / 5040))))
    cos = 1.0 + x2 * (-0.5 + x2 * (1.0 / 24 + x2 * (-1.0 / 720 + x2 * (1.0 / 40320))))
    swap = (quad & 1) == 1
    a = jnp.where(swap, sin, cos)
    b = jnp.where(swap, cos, sin)
    a = jnp.where((quad == 1) | (quad == 2), -a, a)
    b = jnp.where(quad >= 2, -b, b)
    return a, b


def pair_kernel(
    n, snake, spec_ref, count_ref, beam_ref, table_ref,
    gathered, out_half, x_rows, p_rows, own, lhs_x, lhs_p, level_own, level_all,
    cube, stacked, picks, sums, beam_out, c_low, s_low, c_high, s_high, count_pad,
    l_send, l_recv, r_send, r_recv, h_send, h_recv, b_send, b_recv,
):
    segs, stations, spread = spec_ref.shape
    half = spread // 2
    chunks = half // 2 // BINS
    tiles = stations // ROWS
    both = 2 * stations
    chips = n // 2
    far = chips // 2
    groups = chips // 4
    size = segs * stations
    depth = LEVELS * 8
    band = lax.axis_index("band")
    me = lax.axis_index("blk")
    core = me % 2
    chip = me // 2
    place = place_of(chip, chips, snake)
    left = chip_of((place + chips - 1) % chips, chips, snake) * 2
    right = chip_of((place + 1) % chips, chips, snake) * 2
    sibling = chip * 2 + 1 - core

    barrier = pltpu.get_barrier_semaphore()
    for other in (left, left + 1, right, right + 1, sibling):
        pl.semaphore_signal(
            barrier, inc=1, device_id=(band, other), device_id_type=pl.DeviceIdType.MESH
        )

    def remote(src, dst, send, recv, other):
        return pltpu.make_async_remote_copy(
            src_ref=src, dst_ref=dst, send_sem=send, recv_sem=recv,
            device_id=(band, other), device_id_type=pl.DeviceIdType.MESH,
        )

    def rows_of(c):
        return pl.ds(0, 128 if c == 0 else size)

    def swap_copy(c, q):
        return remote(
            out_half.at[c, rows_of(c)], gathered.at[c, 0, q, rows_of(c)],
            h_send.at[c], h_recv.at[c], sibling,
        )

    def first_copies(c, q):
        same, cross = (gathered.at[c, 0, core, rows_of(c)], out_half.at[c, rows_of(c)])
        copies = []
        for other, slot, send, recv in (
            (left, 1, l_send, l_recv), (right, chips - 1, r_send, r_recv)
        ):
            for k, src in enumerate((same, cross)):
                which = core if k == 0 else 1 - core
                copies.append(remote(
                    src, gathered.at[c, slot, q, rows_of(c)],
                    send.at[c, 0, k], recv.at[c, 0, q], other + which,
                ))
        return copies

    def arrived_first(c):
        for slot, recv, send, other in (
            (1, l_recv, l_send, left), (chips - 1, r_recv, r_send, right)
        ):
            for q in range(2):
                remote(
                    out_half.at[c, rows_of(c)], gathered.at[c, slot, q, rows_of(c)],
                    send.at[c, 0, q], recv.at[c, 0, q], other,
                ).wait_recv()

    def ring(c, hop, last, first):
        rows = pl.ds(0, 128 if first else size)
        lq = pl.ds(0, 1) if last else pl.ds(0, 2)
        rq = pl.ds(1, 1) if last else pl.ds(0, 2)
        a = remote(
            gathered.at[c, hop - 1, lq, rows], gathered.at[c, hop, lq, rows],
            l_send.at[c, hop - 1, 0], l_recv.at[c, hop - 1, 0], left + core,
        )
        b = remote(
            gathered.at[c, chips - hop + 1, rq, rows], gathered.at[c, chips - hop, rq, rows],
            r_send.at[c, hop - 1, 0], r_recv.at[c, hop - 1, 0], right + core,
        )
        return a, b

    def ring_do(c, hop, what):
        def go(last, first):
            def fn():
                for copy in ring(c, hop, last, first):
                    getattr(copy, what)()
            return fn
        if isinstance(c, int) and isinstance(hop, int):
            go(hop == far, c == 0)()
            return
        for last in (False, True):
            for first in (False, True):
                right_hop = (hop == far) if last else (hop < far)
                right_part = (c == 0) if first else (c > 0)
                pl.when(right_hop & right_part)(go(last, first))

    def advance(c, hop):
        if isinstance(hop, int) and hop == 1:
            arrived_first(c)
        else:
            ring_do(c, hop, "wait_recv")
        when(hop < far, lambda: ring_do(c, hop + 1, "start"))

    lane24 = lane_ids(stations)
    low24 = lane24 < 64

    def piece(s, c, which):
        at = pl.multiple_of(which * (half // 2) + (c // 2) * LANES, LANES)
        re = spec_ref[s, :, pl.ds(at, LANES)].astype(F32)
        im = spec_ref[s, :, pl.ds(half + at, LANES)].astype(F32)
        if c % 2 == 0:
            return jnp.where(low24, re, pltpu.roll(im, 64, 1))
        return jnp.where(low24, pltpu.roll(re, 64, 1), im)

    count_pad[...] = jnp.zeros_like(count_pad)
    count_pad[0:segs, 0:stations] = count_ref[...].astype(F32)
    counted = count_pad[...].T
    seg24 = (lane24 & 7) >> 1
    plane = jnp.zeros((stations, LANES), F32)
    for s in range(segs):
        plane = jnp.where(seg24 == s, counted[:stations, s : s + 1], plane)
    pad = jnp.zeros((128 - size - stations, LANES), F32)

    for c in range(chunks):
        away = [piece(s, c, 1 - core) for s in range(segs)]
        home = [piece(s, c, core) for s in range(segs)]
        if c == 0:
            away += [plane, pad]
            home += [plane, pad]
        out_half[c, rows_of(c), :] = jnp.concatenate(away, 0).astype(BF16)
        gathered[c, 0, core, rows_of(c), :] = jnp.concatenate(home, 0).astype(BF16)
        if c == 0:
            pl.semaphore_wait(barrier, 5)
        swap_copy(c, core).start()
        for copy in first_copies(c, core):
            copy.start()

    low = row_ids(16, LAG)
    c_low[...], s_low[...] = cos_sin(low, 16)
    high = row_ids(half // 16, LAG) * 16
    c_high[...], s_high[...] = cos_sin(high, half // 16)

    def table_rows(h, carry):
        a = c_high[pl.ds(h, 1), :]
        b = s_high[pl.ds(h, 1), :]
        at = (h // 2) * 64 + (h % 2) * 16
        table_ref[pl.ds(pl.multiple_of(at, 16), 16), :] = (
            a * c_low[...] - b * s_low[...]
        ).astype(BF16)
        table_ref[pl.ds(pl.multiple_of(at + 32, 16), 16), :] = (
            b * c_low[...] + a * s_low[...]
        ).astype(BF16)
        return carry

    lax.fori_loop(0, half // 16, table_rows, 0, unroll=2)

    def sum_picks(e):
        lane = lax.broadcasted_iota(jnp.int32, (LANES, ROWS * n), 0)
        col = lax.broadcasted_iota(jnp.int32, (LANES, ROWS * n), 1)
        d = (lane >> 4) & 3
        off = jnp.where(
            d == 0, (chips - 2 * e) % chips,
            jnp.where(d == 1, 2 * e + 1, jnp.where(d == 2, chips - 2 * e - 1, 2 * e + 2)),
        )
        where = place + off
        where = jnp.where(where >= chips, where - chips, where)
        block = 2 * chip_of(where, chips, snake) + ((lane >> 3) & 1)
        low = lane < 64
        for q in range(2):
            k = block - (2 * chip + q)
            k = jnp.where(k < 0, k + n, k)
            for u in range(ROWS):
                hit = col == u * n + k
                at = slice(u * LANES, (u + 1) * LANES)
                picks[q, at, : ROWS * n] = jnp.where(hit & low, 1.0, 0.0).astype(BF16)
                picks[q, at, ROWS * n :] = jnp.where(hit & ~low, 1.0, 0.0).astype(BF16)

    sums[...] = jnp.zeros_like(sums)

    lane8 = lane_ids(ROWS)
    lane48 = lane_ids(both)
    row128 = row_ids(LANES)

    def wait_swap(c):
        remote(
            out_half.at[c, rows_of(c)], gathered.at[c, 0, 1 - core, rows_of(c)],
            h_send.at[c], h_recv.at[c], sibling,
        ).wait_recv()

    def eight(c, slot, q, row):
        base = row // 16 * 16
        return gathered[c, slot, q, pl.ds(base, 16), :].astype(F32)[row - base : row - base + 8]

    def own_rows(c, start):
        return jnp.concatenate(
            [eight(c, 0, q, start + t * ROWS) for t in range(tiles) for q in range(2)], 0
        )

    for c in range(chunks):
        wait_swap(c)
    own_count = own_rows(0, size)
    levels = jnp.where(own_count >= ((lane48 >> 3) + 1).astype(F32), 1.0, 0.0)
    level_own[...] = jnp.concatenate([levels, levels], 0)

    def prepare_own(c):
        planes = [own_rows(c, s * stations) for s in range(segs)]
        seg8 = (lane8 & 7) >> 1
        part8 = lane8 & 1
        sign = (1 - 2 * part8).astype(F32)
        swap = lane8 ^ 1
        for g in range(BINS // 16):
            at = part8 * 64 + g * 16 + (lane8 >> 3)
            parts = [[], [], [], []]
            for r in range(0, both, ROWS):
                re = None
                for s in range(segs):
                    v = jnp.take_along_axis(planes[s][r : r + ROWS], at, axis=1)
                    re = v if s == 0 else jnp.where(seg8 == s, v, re)
                im = jnp.take_along_axis(re, swap, axis=1) * sign
                inv = lax.rsqrt(re * re + im * im + 0.25)
                parts[0].append(re)
                parts[1].append(im)
                parts[2].append(re * inv)
                parts[3].append(im * inv)
            own[g] = jnp.concatenate(parts[0] + parts[1] + parts[2] + parts[3], 0).astype(BF16)

        source = row_ids(LANES, 2 * LANES)
        column = lax.broadcasted_iota(jnp.int32, (LANES, 2 * LANES), 1)
        wanted = (column & 7) + 8 * (column >> 7)

        def spread_one(g, carry):
            for f in range(0, 16, 2):
                copy = jnp.where(source == wanted + 8 * f, 1.0, 0.0).astype(BF16)
                wide = jnp.dot(own[g], copy, preferred_element_type=F32)
                for x in range(2):
                    for k, lhs in enumerate((lhs_x, lhs_p)):
                        part = wide[k * 2 * both : (k + 1) * 2 * both, x * LANES : (x + 1) * LANES]
                        lhs[c, g * 16 + f + x] = (part * level_own[...]).astype(BF16)
            return carry

        lax.fori_loop(0, BINS // 16, spread_one, 0)

    def slots_of(e):
        return ((chips - 2 * e) % chips, 2 * e + 1, chips - 2 * e - 1, 2 * e + 2)

    def stack(c, e, start, part):
        slots = slots_of(e)
        rows = [
            eight(c, slots[d], q, start + t * ROWS)
            for t in ((0, 1) if part == 0 else (2,)) for d in range(4) for q in range(2)
        ]
        if part == 1:
            rows.append(jnp.zeros((64, LANES), F32))
        return jnp.concatenate(rows, 0).T

    def prepare_group(e):
        sum_picks(e)
        for v in range(2):
            turned = stack(0, e, size, v)
            level_all[:, v * LANES : (v + 1) * LANES] = jnp.where(
                turned >= ((row128 >> 3) + 1).astype(F32), 1.0, 0.0
            )[:depth].astype(BF16)
            total = jnp.zeros((both, LANES), F32)
            mine = own_rows(0, size)
            for s in range(segs):
                total = total + jnp.minimum(mine[:, 2 * s : 2 * s + 1], turned[2 * s : 2 * s + 1, :])
            total = jnp.maximum(total, 1.0)
            share = 1.0 / total
            cube[:, v * LANES : (v + 1) * LANES] = share * share * share

    def prepare_all(c, e):
        for s in range(segs):
            for v in range(2):
                turned = stack(c, e, s * stations, v)
                re, im = turned[:64], turned[64:]
                inv = lax.rsqrt(re * re + im * im + 0.25)
                x_rows[v, (2 * s) * XROWS : (2 * s) * XROWS + 64, :] = re
                x_rows[v, (2 * s + 1) * XROWS : (2 * s + 1) * XROWS + 64, :] = im
                p_rows[v, (2 * s) * XROWS : (2 * s) * XROWS + 64, :] = re * inv
                p_rows[v, (2 * s + 1) * XROWS : (2 * s + 1) * XROWS + 64, :] = im * inv

    low48 = lane48 < 64

    def one_bin(c, at):
        products = []
        for lhs, rows in ((lhs_x, x_rows), (lhs_p, p_rows)):
            cols = []
            for v in range(2):
                x8 = rows[v, pl.ds(at, 8, stride=XROWS), :]
                x16 = jnp.concatenate([x8, x8], 0).astype(BF16)
                cols.append(jnp.concatenate(
                    [x16 * level_all[k : k + 16, v * LANES : (v + 1) * LANES] for k in range(0, depth, 16)], 0
                ))
            products.append(jnp.dot(
                lhs[c, at, :, :depth], jnp.concatenate(cols, 1), preferred_element_type=F32
            ))
        cross, coh = products
        hr, hi = coh[:both], coh[both:]
        factor = (hr * hr + hi * hi) * cube[...]
        sums = []
        for part in (cross[:both] * factor, cross[both:] * factor):
            total = part[:, :LANES] + part[:, LANES:]
            sums.append(total + pltpu.roll(total, 64, 1))
        return sums

    def two_bins(c, at):
        first = one_bin(c, at)
        second = one_bin(c, at + PAIRS)
        for part in range(2):
            stacked[pl.ds(part * PAIRS + at, both, stride=ZROWS), :] = jnp.where(
                low48, first[part], second[part]
            )

    def beam_copy(c, h):
        return remote(beam_out.at[c], beam_ref.at[h, c], b_send.at[c], b_recv.at[c], sibling)

    def reduce_beams(c, e):
        wide = ROWS * n
        for o in range(2):
            q = core if o == 0 else 1 - core
            z = jnp.concatenate([
                jnp.concatenate([
                    stacked[
                        pl.ds(pl.multiple_of((t * 16 + q * 8 + u) * ZROWS, 8), 2 * PAIRS), :
                    ].astype(BF16)
                    for u in range(ROWS)
                ], 1)
                for t in range(tiles)
            ], 0)
            sums[c, o] = sums[c, o] + jnp.dot(z, picks[q], preferred_element_type=F32)

        @pl.when(e == groups - 1)
        def _():
            for o in range(2):
                for t in range(tiles):
                    rows = slice(t * 2 * PAIRS, (t + 1) * 2 * PAIRS)
                    turned = jnp.concatenate(
                        [sums[c, o, rows, :wide], sums[c, o, rows, wide:]], 0
                    ).T.astype(BF16)
                    at = pl.ds(t * wide, wide)
                    if o == 0:
                        beam_ref[core, c, at, :] = turned
                    else:
                        beam_out[c, at, :] = turned
            beam_copy(c, core).start()

    for c in range(chunks):
        prepare_own(c)
        if c > 0:
            advance(c - 1, 1)
    advance(chunks - 1, 1)
    advance(0, 2)

    def work(step, carry):
        e = step // chunks
        c = step % chunks

        @pl.when(c == 0)
        def _():
            prepare_group(e)

        prepare_all(c, e)

        def forward(index):
            @pl.when(index < far * chunks)
            def _():
                advance(index % chunks, index // chunks + 1)

        forward(chunks + 1 + 2 * step)
        for f in range(PAIRS):
            two_bins(c, f)
        forward(chunks + 2 + 2 * step)
        reduce_beams(c, e)
        return carry

    lax.fori_loop(0, groups * chunks, work, 0)

    for c in range(chunks):
        swap_copy(c, core).wait_send()
        for copy in first_copies(c, core):
            copy.wait_send()

    def drain(index, carry):
        ring_do(index % chunks, index // chunks + 2, "wait_send")
        return carry

    lax.fori_loop(0, (far - 1) * chunks, drain, 0)
    for c in range(chunks):
        beam_copy(c, core).wait_send()
        beam_copy(c, 1 - core).wait_recv()


def pair_beams(spectra, counts, n, snake):
    segs, stations, spread = spectra.shape
    half = spread // 2
    chunks = half // 2 // BINS
    chips = n // 2
    far = chips // 2
    tiles = stations // ROWS
    both = 2 * stations
    dma = pltpu.SemaphoreType.DMA
    pairs = n * stations * stations * half
    return pl.pallas_call(
        functools.partial(pair_kernel, n, snake),
        out_shape=(
            jax.ShapeDtypeStruct((2, chunks, stations * n, LANES), BF16),
            jax.ShapeDtypeStruct((spread, LAG), BF16),
        ),
        in_specs=[pl.BlockSpec(memory_space=pltpu.VMEM)] * 2,
        out_specs=[pl.BlockSpec(memory_space=pltpu.VMEM)] * 2,
        scratch_shapes=[
            pltpu.VMEM((chunks, chips, 2, 128, LANES), BF16),
            pltpu.VMEM((chunks, 128, LANES), BF16),
            pltpu.VMEM((2, 8 * XROWS, LANES), F32),
            pltpu.VMEM((2, 8 * XROWS, LANES), F32),
            pltpu.VMEM((BINS // 16, 4 * both, LANES), BF16),
            pltpu.VMEM((chunks, BINS, 2 * both, LANES), BF16),
            pltpu.VMEM((chunks, BINS, 2 * both, LANES), BF16),
            pltpu.VMEM((2 * both, LANES), F32),
            pltpu.VMEM((LEVELS * 8, 2 * LANES), BF16),
            pltpu.VMEM((both, 2 * LANES), F32),
            pltpu.VMEM((both * ZROWS, LANES), F32),
            pltpu.VMEM((2, ROWS * LANES, 2 * ROWS * n), BF16),
            pltpu.VMEM((chunks, 2, tiles * 2 * PAIRS, 2 * ROWS * n), F32),
            pltpu.VMEM((chunks, stations * n, LANES), BF16),
            pltpu.VMEM((16, LAG), F32), pltpu.VMEM((16, LAG), F32),
            pltpu.VMEM((half // 16, LAG), F32), pltpu.VMEM((half // 16, LAG), F32),
            pltpu.VMEM((LANES, LANES), F32),
            dma((chunks, far, 2)), dma((chunks, far, 2)), dma((chunks, far, 2)), dma((chunks, far, 2)),
            dma((chunks,)), dma((chunks,)), dma((chunks,)), dma((chunks,)),
        ],
        compiler_params=pltpu.CompilerParams(
            collective_id=0, has_side_effects=True, vmem_limit_bytes=(30 + n * 3 // 8) * 1024 * 1024
        ),
        cost_estimate=pl.CostEstimate(
            flops=66 * pairs, bytes_accessed=2 * spectra.size, transcendentals=0
        ),
        name="pair_beams",
    )(spectra, counts)


def lag_kernel(beam_ref, table_ref, out_ref):
    halves, chunks = beam_ref.shape[:2]
    rows = jnp.concatenate(
        [beam_ref[h, c] for h in range(halves) for c in range(chunks)], 1
    )
    trace = jnp.dot(rows, table_ref[...], preferred_element_type=F32)
    values = trace.astype(BF16).astype(F32)
    scale = jnp.sqrt(jnp.mean(values * values, -1, keepdims=True) + 1e-06)
    out_ref[...] = (values / scale).astype(BF16)


def lag_traces(beams, table):
    halves, chunks, rows, _ = beams.shape
    block = 128
    return pl.pallas_call(
        lag_kernel,
        grid=(rows // block,),
        out_shape=jax.ShapeDtypeStruct((rows, LAG), BF16),
        in_specs=[
            pl.BlockSpec((halves, chunks, block, LANES), lambda i: (0, 0, i, 0)),
            pl.BlockSpec(table.shape, lambda i: (0, 0)),
        ],
        out_specs=pl.BlockSpec((block, LAG), lambda i: (i, 0)),
        compiler_params=pltpu.CompilerParams(vmem_limit_bytes=32 * 1024 * 1024),
        name="lag_traces",
    )(beams, table)


def shards(snake, spectra, counts):
    n = lax.axis_size("blk")
    stations, segs, spread = spectra.shape
    beams, table = pair_beams(spectra.transpose(1, 0, 2), counts.T, n, snake)
    out = lag_traces(beams, table)
    return out.reshape(stations, n, LAG)


def solution(mesh):
    snake = mesh.shape["blk"] == 16
    return jax.shard_map(
        functools.partial(shards, snake),
        mesh=mesh,
        in_specs=(P(("band", "blk"), None, None), P(("band", "blk"), None)),
        out_specs=P(("band", "blk"), None, None),
        check_vma=False,
    )
```

```python
import functools
import math

import jax
import jax.numpy as jnp
from jax import lax
from jax.experimental import pallas as pl
from jax.experimental.pallas import tpu as pltpu
from jax.sharding import PartitionSpec as P

LAG = 1024
LANES = 128
ROWS = 8
LEVELS = 12
BINS = 64
ZROWS = 72
XROWS = 72
PAIRS = BINS // 2
F32 = jnp.float32
BF16 = jnp.bfloat16


def chip_of(place, chips, snake):
    if not snake:
        return place
    return jnp.where(place < chips // 2, 2 * place, 2 * (chips - 1 - place) + 1)


def place_of(chip, chips, snake):
    if not snake:
        return chip
    return jnp.where(chip % 2 == 0, chip // 2, chips - 1 - chip // 2)


def when(pred, fn):
    if isinstance(pred, bool):
        if pred:
            fn()
    else:
        pl.when(pred)(fn)


def lane_ids(rows):
    return lax.broadcasted_iota(jnp.int32, (rows, LANES), 1)


def row_ids(rows, lanes=LANES):
    return lax.broadcasted_iota(jnp.int32, (rows, lanes), 0)


def cos_sin(bins, rows):
    taps = lax.broadcasted_iota(jnp.int32, (rows, LAG), 1) - LAG // 2
    phase = (bins * taps) & (LAG - 1)
    quad = ((phase + LAG // 8) >> 8) & 3
    x = (((phase + LAG // 8) & (LAG // 4 - 1)) - LAG // 8).astype(F32) * (2.0 * math.pi / LAG)
    x2 = x * x
    sin = x * (1.0 + x2 * (-1.0 / 6 + x2 * (1.0 / 120 - x2 * (1.0 / 5040))))
    cos = 1.0 + x2 * (-0.5 + x2 * (1.0 / 24 + x2 * (-1.0 / 720 + x2 * (1.0 / 40320))))
    swap = (quad & 1) == 1
    a = jnp.where(swap, sin, cos)
    b = jnp.where(swap, cos, sin)
    a = jnp.where((quad == 1) | (quad == 2), -a, a)
    b = jnp.where(quad >= 2, -b, b)
    return a, b


def pair_kernel(
    n, snake, spec_ref, count_hbm, beam_ref, table_ref, count_ref, count_sem,
    gathered, out_half, x_rows, p_rows, own, lhs_x, lhs_p, level_own, level_all,
    cube, stacked_a, stacked_b, picks, sums, beam_out, c_low, s_low, c_high, s_high, count_pad,
    l_send, l_recv, r_send, r_recv, h_send, h_recv, b_send, b_recv,
):
    segs, stations, spread = spec_ref.shape
    half = spread // 2
    chunks = half // 2 // BINS
    tiles = stations // ROWS
    both = 2 * stations
    chips = n // 2
    far = chips // 2
    groups = chips // 4
    size = segs * stations
    depth = LEVELS * 8
    band = lax.axis_index("band")
    me = lax.axis_index("blk")
    core = me % 2
    chip = me // 2
    place = place_of(chip, chips, snake)
    left = chip_of((place + chips - 1) % chips, chips, snake) * 2
    right = chip_of((place + 1) % chips, chips, snake) * 2
    sibling = chip * 2 + 1 - core

    counting = pltpu.make_async_copy(count_hbm, count_ref, count_sem)
    counting.start()
    barrier = pltpu.get_barrier_semaphore()
    for other in (left, left + 1, right, right + 1, sibling):
        pl.semaphore_signal(
            barrier, inc=1, device_id=(band, other), device_id_type=pl.DeviceIdType.MESH
        )

    def remote(src, dst, send, recv, other):
        return pltpu.make_async_remote_copy(
            src_ref=src, dst_ref=dst, send_sem=send, recv_sem=recv,
            device_id=(band, other), device_id_type=pl.DeviceIdType.MESH,
        )

    def rows_of(c):
        return pl.ds(0, 128 if c == 0 else size)

    def swap_copy(c, q):
        return remote(
            out_half.at[c, rows_of(c)], gathered.at[c, 0, q, rows_of(c)],
            h_send.at[c], h_recv.at[c], sibling,
        )

    def first_copies(c, q):
        same, cross = (gathered.at[c, 0, core, rows_of(c)], out_half.at[c, rows_of(c)])
        copies = []
        for other, slot, send, recv in (
            (left, 1, l_send, l_recv), (right, chips - 1, r_send, r_recv)
        ):
            for k, src in enumerate((same, cross)):
                which = core if k == 0 else 1 - core
                copies.append(remote(
                    src, gathered.at[c, slot, q, rows_of(c)],
                    send.at[c, 0, k], recv.at[c, 0, q], other + which,
                ))
        return copies

    def arrived_first(c):
        for slot, recv, send, other in (
            (1, l_recv, l_send, left), (chips - 1, r_recv, r_send, right)
        ):
            for q in range(2):
                remote(
                    out_half.at[c, rows_of(c)], gathered.at[c, slot, q, rows_of(c)],
                    send.at[c, 0, q], recv.at[c, 0, q], other,
                ).wait_recv()

    def ring(c, hop, last, first):
        rows = pl.ds(0, 128 if first else size)
        lq = pl.ds(0, 1) if last else pl.ds(0, 2)
        rq = pl.ds(1, 1) if last else pl.ds(0, 2)
        a = remote(
            gathered.at[c, hop - 1, lq, rows], gathered.at[c, hop, lq, rows],
            l_send.at[c, hop - 1, 0], l_recv.at[c, hop - 1, 0], left + core,
        )
        b = remote(
            gathered.at[c, chips - hop + 1, rq, rows], gathered.at[c, chips - hop, rq, rows],
            r_send.at[c, hop - 1, 0], r_recv.at[c, hop - 1, 0], right + core,
        )
        return a, b

    def ring_do(c, hop, what):
        def go(last, first):
            def fn():
                for copy in ring(c, hop, last, first):
                    getattr(copy, what)()
            return fn
        if isinstance(c, int) and isinstance(hop, int):
            go(hop == far, c == 0)()
            return
        for last in (False, True):
            for first in (False, True):
                right_hop = (hop == far) if last else (hop < far)
                right_part = (c == 0) if first else (c > 0)
                pl.when(right_hop & right_part)(go(last, first))

    def advance(c, hop):
        if isinstance(hop, int) and hop == 1:
            arrived_first(c)
        else:
            ring_do(c, hop, "wait_recv")
        when(hop < far, lambda: ring_do(c, hop + 1, "start"))

    lane24 = lane_ids(stations)
    low24 = lane24 < 64

    def piece(s, c, which):
        at = pl.multiple_of(which * (half // 2) + (c // 2) * LANES, LANES)
        re = spec_ref[s, :, pl.ds(at, LANES)].astype(F32)
        im = spec_ref[s, :, pl.ds(half + at, LANES)].astype(F32)
        if c % 2 == 0:
            return jnp.where(low24, re, pltpu.roll(im, 64, 1))
        return jnp.where(low24, pltpu.roll(re, 64, 1), im)

    count_pad[...] = jnp.zeros_like(count_pad)
    counting.wait()
    count_pad[0:segs, 0:stations] = count_ref[...].astype(F32)
    counted = count_pad[...].T
    seg24 = (lane24 & 7) >> 1
    plane = jnp.zeros((stations, LANES), F32)
    for s in range(segs):
        plane = jnp.where(seg24 == s, counted[:stations, s : s + 1], plane)
    pad = jnp.zeros((128 - size - stations, LANES), F32)

    for c in range(chunks):
        away = [piece(s, c, 1 - core) for s in range(segs)]
        home = [piece(s, c, core) for s in range(segs)]
        if c == 0:
            away += [plane, pad]
            home += [plane, pad]
        out_half[c, rows_of(c), :] = jnp.concatenate(away, 0).astype(BF16)
        gathered[c, 0, core, rows_of(c), :] = jnp.concatenate(home, 0).astype(BF16)
        if c == 0:
            pl.semaphore_wait(barrier, 5)
        swap_copy(c, core).start()
        for copy in first_copies(c, core):
            copy.start()

    low = row_ids(16, LAG)
    c_low[...], s_low[...] = cos_sin(low, 16)
    high = row_ids(half // 16, LAG) * 16
    c_high[...], s_high[...] = cos_sin(high, half // 16)

    def table_rows(h, carry):
        a = c_high[pl.ds(h, 1), :]
        b = s_high[pl.ds(h, 1), :]
        at = (h // 2) * 64 + (h % 2) * 16
        table_ref[pl.ds(pl.multiple_of(at, 16), 16), :] = (
            a * c_low[...] - b * s_low[...]
        ).astype(BF16)
        table_ref[pl.ds(pl.multiple_of(at + 32, 16), 16), :] = (
            b * c_low[...] + a * s_low[...]
        ).astype(BF16)
        return carry

    lax.fori_loop(0, half // 16, table_rows, 0, unroll=2)

    def sum_picks(e):
        lane = lax.broadcasted_iota(jnp.int32, (LANES, ROWS * n), 0)
        col = lax.broadcasted_iota(jnp.int32, (LANES, ROWS * n), 1)
        d = (lane >> 4) & 3
        off = jnp.where(
            d == 0, (chips - 2 * e) % chips,
            jnp.where(d == 1, 2 * e + 1, jnp.where(d == 2, chips - 2 * e - 1, 2 * e + 2)),
        )
        where = place + off
        where = jnp.where(where >= chips, where - chips, where)
        block = 2 * chip_of(where, chips, snake) + ((lane >> 3) & 1)
        low = lane < 64
        for q in range(2):
            k = block - (2 * chip + q)
            k = jnp.where(k < 0, k + n, k)
            for u in range(ROWS):
                hit = col == u * n + k
                at = slice(u * LANES, (u + 1) * LANES)
                picks[2 * (e % 2) + q, at, : ROWS * n] = jnp.where(hit & low, 1.0, 0.0).astype(BF16)
                picks[2 * (e % 2) + q, at, ROWS * n :] = jnp.where(hit & ~low, 1.0, 0.0).astype(BF16)

    sums[...] = jnp.zeros_like(sums)
    stacked_b[...] = jnp.zeros_like(stacked_b)

    lane8 = lane_ids(ROWS)
    lane48 = lane_ids(both)
    row128 = row_ids(LANES)

    def wait_swap(c):
        remote(
            out_half.at[c, rows_of(c)], gathered.at[c, 0, 1 - core, rows_of(c)],
            h_send.at[c], h_recv.at[c], sibling,
        ).wait_recv()

    def eight(c, slot, q, row):
        base = row // 16 * 16
        return gathered[c, slot, q, pl.ds(base, 16), :].astype(F32)[row - base : row - base + 8]

    def own_rows(c, start):
        return jnp.concatenate(
            [eight(c, 0, q, start + t * ROWS) for t in range(tiles) for q in range(2)], 0
        )

    for c in range(chunks):
        wait_swap(c)
    own_count = own_rows(0, size)
    levels = jnp.where(own_count >= ((lane48 >> 3) + 1).astype(F32), 1.0, 0.0)
    level_own[...] = jnp.concatenate([levels, levels], 0)

    def prepare_own(c):
        planes = [own_rows(c, s * stations) for s in range(segs)]
        seg8 = (lane8 & 7) >> 1
        part8 = lane8 & 1
        sign = (1 - 2 * part8).astype(F32)
        swap = lane8 ^ 1
        for g in range(BINS // 16):
            at = part8 * 64 + g * 16 + (lane8 >> 3)
            parts = [[], [], [], []]
            for r in range(0, both, ROWS):
                re = None
                for s in range(segs):
                    v = jnp.take_along_axis(planes[s][r : r + ROWS], at, axis=1)
                    re = v if s == 0 else jnp.where(seg8 == s, v, re)
                im = jnp.take_along_axis(re, swap, axis=1) * sign
                inv = lax.rsqrt(re * re + im * im + 0.25)
                parts[0].append(re)
                parts[1].append(im)
                parts[2].append(re * inv)
                parts[3].append(im * inv)
            own[g] = jnp.concatenate(parts[0] + parts[1] + parts[2] + parts[3], 0).astype(BF16)

        source = row_ids(LANES, 2 * LANES)
        column = lax.broadcasted_iota(jnp.int32, (LANES, 2 * LANES), 1)
        wanted = (column & 7) + 8 * (column >> 7)

        def spread_one(g, carry):
            for f in range(0, 16, 2):
                copy = jnp.where(source == wanted + 8 * f, 1.0, 0.0).astype(BF16)
                wide = jnp.dot(own[g], copy, preferred_element_type=F32)
                for x in range(2):
                    for k, lhs in enumerate((lhs_x, lhs_p)):
                        part = wide[k * 2 * both : (k + 1) * 2 * both, x * LANES : (x + 1) * LANES]
                        lhs[c, g * 16 + f + x] = (part * level_own[...]).astype(BF16)
            return carry

        lax.fori_loop(0, BINS // 16, spread_one, 0, unroll=True)

    def slots_of(e):
        return ((chips - 2 * e) % chips, 2 * e + 1, chips - 2 * e - 1, 2 * e + 2)

    def stack(c, e, start, part):
        slots = slots_of(e)
        rows = [
            eight(c, slots[d], q, start + t * ROWS)
            for t in ((0, 1) if part == 0 else (2,)) for d in range(4) for q in range(2)
        ]
        if part == 1:
            rows.append(jnp.zeros((64, LANES), F32))
        return jnp.concatenate(rows, 0).T

    def prepare_group(e):
        sum_picks(e)
        for v in range(2):
            turned = stack(0, e, size, v)
            level_all[:, v * LANES : (v + 1) * LANES] = jnp.where(
                turned >= ((row128 >> 3) + 1).astype(F32), 1.0, 0.0
            )[:depth].astype(BF16)
            total = jnp.zeros((both, LANES), F32)
            mine = own_rows(0, size)
            for s in range(segs):
                total = total + jnp.minimum(mine[:, 2 * s : 2 * s + 1], turned[2 * s : 2 * s + 1, :])
            total = jnp.maximum(total, 1.0)
            share = 1.0 / total
            cube[:, v * LANES : (v + 1) * LANES] = share * share * share

    def prepare_all(c, e):
        for s in range(segs):
            for v in range(2):
                turned = stack(c, e, s * stations, v)
                re, im = turned[:64], turned[64:]
                inv = lax.rsqrt(re * re + im * im + 0.25)
                x_rows[v, (2 * s) * XROWS : (2 * s) * XROWS + 64, :] = re
                x_rows[v, (2 * s + 1) * XROWS : (2 * s + 1) * XROWS + 64, :] = im
                p_rows[v, (2 * s) * XROWS : (2 * s) * XROWS + 64, :] = re * inv
                p_rows[v, (2 * s + 1) * XROWS : (2 * s + 1) * XROWS + 64, :] = im * inv

    low48 = lane48 < 64

    def one_bin(c, at):
        products = []
        for lhs, rows in ((lhs_x, x_rows), (lhs_p, p_rows)):
            cols = []
            for v in range(2):
                x8 = rows[v, pl.ds(at, 8, stride=XROWS), :]
                x16 = jnp.concatenate([x8, x8], 0).astype(BF16)
                cols.append(jnp.concatenate(
                    [x16 * level_all[k : k + 16, v * LANES : (v + 1) * LANES] for k in range(0, depth, 16)], 0
                ))
            products.append(jnp.dot(
                lhs[c, at, :, :depth], jnp.concatenate(cols, 1), preferred_element_type=F32
            ))
        cross, coh = products
        hr, hi = coh[:both], coh[both:]
        factor = (hr * hr + hi * hi) * cube[...]
        sums = []
        for part in (cross[:both] * factor, cross[both:] * factor):
            total = part[:, :LANES] + part[:, LANES:]
            sums.append(total + pltpu.roll(total, 64, 1))
        return sums

    def two_bins(c, at, stacked):
        first = one_bin(c, at)
        second = one_bin(c, at + PAIRS)
        for part in range(2):
            stacked[pl.ds(part * PAIRS + at, both, stride=ZROWS), :] = jnp.where(
                low48, first[part], second[part]
            )

    def beam_copy(c, h):
        return remote(beam_out.at[c], beam_ref.at[h, c], b_send.at[c], b_recv.at[c], sibling)

    def reduce_beams(c, e, stacked):
        wide = ROWS * n
        for o in range(2):
            q = core if o == 0 else 1 - core
            z = jnp.concatenate([
                jnp.concatenate([
                    stacked[
                        pl.ds(pl.multiple_of((t * 16 + q * 8 + u) * ZROWS, 8), 2 * PAIRS), :
                    ].astype(BF16)
                    for u in range(ROWS)
                ], 1)
                for t in range(tiles)
            ], 0)
            sums[c, o] = sums[c, o] + jnp.dot(z, picks[2 * (e % 2) + q], preferred_element_type=F32)

    def finish(c, e):
        wide = ROWS * n

        def send():
            for o in range(2):
                for t in range(tiles):
                    rows = slice(t * 2 * PAIRS, (t + 1) * 2 * PAIRS)
                    turned = jnp.concatenate(
                        [sums[c, o, rows, :wide], sums[c, o, rows, wide:]], 0
                    ).T.astype(BF16)
                    at = pl.ds(t * wide, wide)
                    if o == 0:
                        beam_ref[core, c, at, :] = turned
                    else:
                        beam_out[c, at, :] = turned
            beam_copy(c, core).start()

        when(e == groups - 1, send)

    for c in range(chunks):
        prepare_own(c)
        if c > 0:
            advance(c - 1, 1)
    advance(chunks - 1, 1)
    advance(0, 2)

    def work(step, now, before):
        e = step // chunks
        c = step % chunks

        @pl.when(c == 0)
        def _():
            prepare_group(e)

        prepare_all(c, e)

        def forward(index):
            @pl.when(index < far * chunks)
            def _():
                advance(index % chunks, index // chunks + 1)

        forward(chunks + 1 + 2 * step)
        last = jnp.maximum(step - 1, 0)
        reduce_beams(last % chunks, last // chunks, before)
        for f in range(PAIRS):
            two_bins(c, f, now)
        forward(chunks + 2 + 2 * step)
        finish(last % chunks, last // chunks)

    def double(x, carry):
        work(2 * x, stacked_a, stacked_b)
        work(2 * x + 1, stacked_b, stacked_a)
        return carry

    lax.fori_loop(0, groups * chunks // 2, double, 0)
    reduce_beams(chunks - 1, groups - 1, stacked_b)
    finish(chunks - 1, groups - 1)

    for c in range(chunks):
        swap_copy(c, core).wait_send()
        for copy in first_copies(c, core):
            copy.wait_send()

    def drain(index, carry):
        ring_do(index % chunks, index // chunks + 2, "wait_send")
        return carry

    lax.fori_loop(0, (far - 1) * chunks, drain, 0)
    for c in range(chunks):
        beam_copy(c, core).wait_send()
        beam_copy(c, 1 - core).wait_recv()


def pair_beams(spectra, counts, n, snake):
    segs, stations, spread = spectra.shape
    half = spread // 2
    chunks = half // 2 // BINS
    chips = n // 2
    far = chips // 2
    tiles = stations // ROWS
    both = 2 * stations
    dma = pltpu.SemaphoreType.DMA
    pairs = n * stations * stations * half
    return pl.pallas_call(
        functools.partial(pair_kernel, n, snake),
        out_shape=(
            jax.ShapeDtypeStruct((2, chunks, stations * n, LANES), BF16),
            jax.ShapeDtypeStruct((spread, LAG), BF16),
        ),
        in_specs=[pl.BlockSpec(memory_space=pltpu.VMEM), pl.BlockSpec(memory_space=pl.ANY)],
        out_specs=[pl.BlockSpec(memory_space=pltpu.VMEM)] * 2,
        scratch_shapes=[
            pltpu.VMEM((segs, stations), jnp.int32),
            dma(()),
            pltpu.VMEM((chunks, chips, 2, 128, LANES), BF16),
            pltpu.VMEM((chunks, 128, LANES), BF16),
            pltpu.VMEM((2, 8 * XROWS, LANES), F32),
            pltpu.VMEM((2, 8 * XROWS, LANES), F32),
            pltpu.VMEM((BINS // 16, 4 * both, LANES), BF16),
            pltpu.VMEM((chunks, BINS, 2 * both, LANES), BF16),
            pltpu.VMEM((chunks, BINS, 2 * both, LANES), BF16),
            pltpu.VMEM((2 * both, LANES), F32),
            pltpu.VMEM((LEVELS * 8, 2 * LANES), BF16),
            pltpu.VMEM((both, 2 * LANES), F32),
            pltpu.VMEM((both * ZROWS, LANES), F32),
            pltpu.VMEM((both * ZROWS, LANES), F32),
            pltpu.VMEM((4, ROWS * LANES, 2 * ROWS * n), BF16),
            pltpu.VMEM((chunks, 2, tiles * 2 * PAIRS, 2 * ROWS * n), F32),
            pltpu.VMEM((chunks, stations * n, LANES), BF16),
            pltpu.VMEM((16, LAG), F32), pltpu.VMEM((16, LAG), F32),
            pltpu.VMEM((half // 16, LAG), F32), pltpu.VMEM((half // 16, LAG), F32),
            pltpu.VMEM((LANES, LANES), F32),
            dma((chunks, far, 2)), dma((chunks, far, 2)), dma((chunks, far, 2)), dma((chunks, far, 2)),
            dma((chunks,)), dma((chunks,)), dma((chunks,)), dma((chunks,)),
        ],
        compiler_params=pltpu.CompilerParams(
            collective_id=0, has_side_effects=True, vmem_limit_bytes=(30 + n * 3 // 8) * 1024 * 1024
        ),
        cost_estimate=pl.CostEstimate(
            flops=66 * pairs, bytes_accessed=2 * spectra.size, transcendentals=0
        ),
        name="pair_beams",
    )(spectra, counts)


def lag_kernel(beam_ref, table_ref, out_ref, block_ref, sems):
    halves, chunks, rows, _ = beam_ref.shape
    copies = []
    for x in range(rows // LANES):
        at = pl.ds(x * LANES, LANES)
        beams = jnp.concatenate(
            [beam_ref[h, c, at, :] for h in range(halves) for c in range(chunks)], 1
        )
        trace = jnp.dot(beams, table_ref[...], preferred_element_type=F32)
        values = trace.astype(BF16).astype(F32)
        scale = jnp.sqrt(jnp.mean(values * values, -1, keepdims=True) + 1e-06)
        block_ref[at, :] = (values / scale).astype(BF16)
        copy = pltpu.make_async_copy(block_ref.at[at], out_ref.at[at], sems.at[x])
        copy.start()
        copies.append(copy)
    for copy in copies:
        copy.wait()


def lag_traces(beams, table):
    rows = beams.shape[2]
    return pl.pallas_call(
        lag_kernel,
        out_shape=jax.ShapeDtypeStruct((rows, LAG), BF16),
        in_specs=[pl.BlockSpec(memory_space=pltpu.VMEM)] * 2,
        out_specs=pl.BlockSpec(memory_space=pl.ANY),
        scratch_shapes=[
            pltpu.VMEM((rows, LAG), BF16), pltpu.SemaphoreType.DMA((rows // LANES,)),
        ],
        compiler_params=pltpu.CompilerParams(vmem_limit_bytes=32 * 1024 * 1024),
        name="lag_traces",
    )(beams, table)


def shards(snake, spectra, counts):
    n = lax.axis_size("blk")
    stations, segs, spread = spectra.shape
    beams, table = pair_beams(spectra.transpose(1, 0, 2), counts.T, n, snake)
    out = lag_traces(beams, table)
    return out.reshape(stations, n, LAG)


def solution(mesh):
    snake = mesh.shape["blk"] == 16
    return jax.shard_map(
        functools.partial(shards, snake),
        mesh=mesh,
        in_specs=(P(("band", "blk"), None, None), P(("band", "blk"), None)),
        out_specs=P(("band", "blk"), None, None),
        check_vma=False,
    )
```

```python
import functools
import math

import jax
import jax.numpy as jnp
from jax import lax
from jax.experimental import pallas as pl
from jax.experimental.pallas import tpu as pltpu
from jax.sharding import PartitionSpec as P

LAG = 1024
LANES = 128
ROWS = 8
LEVELS = 12
BINS = 64
ZROWS = 72
XROWS = 72
PAIRS = BINS // 2
F32 = jnp.float32
BF16 = jnp.bfloat16


def chip_of(place, chips, snake):
    if not snake:
        return place
    return jnp.where(place < chips // 2, 2 * place, 2 * (chips - 1 - place) + 1)


def place_of(chip, chips, snake):
    if not snake:
        return chip
    return jnp.where(chip % 2 == 0, chip // 2, chips - 1 - chip // 2)


def when(pred, fn):
    if isinstance(pred, bool):
        if pred:
            fn()
    else:
        pl.when(pred)(fn)


def lane_ids(rows):
    return lax.broadcasted_iota(jnp.int32, (rows, LANES), 1)


def row_ids(rows, lanes=LANES):
    return lax.broadcasted_iota(jnp.int32, (rows, lanes), 0)


def cos_sin(bins, rows):
    taps = lax.broadcasted_iota(jnp.int32, (rows, LAG), 1) - LAG // 2
    phase = (bins * taps) & (LAG - 1)
    quad = ((phase + LAG // 8) >> 8) & 3
    x = (((phase + LAG // 8) & (LAG // 4 - 1)) - LAG // 8).astype(F32) * (2.0 * math.pi / LAG)
    x2 = x * x
    sin = x * (1.0 + x2 * (-1.0 / 6 + x2 * (1.0 / 120 - x2 * (1.0 / 5040))))
    cos = 1.0 + x2 * (-0.5 + x2 * (1.0 / 24 + x2 * (-1.0 / 720 + x2 * (1.0 / 40320))))
    swap = (quad & 1) == 1
    a = jnp.where(swap, sin, cos)
    b = jnp.where(swap, cos, sin)
    a = jnp.where((quad == 1) | (quad == 2), -a, a)
    b = jnp.where(quad >= 2, -b, b)
    return a, b


def pair_kernel(
    n, snake, spec_ref, count_hbm, beam_ref, table_ref, count_ref, count_sem,
    gathered, out_half, x_rows, p_rows, own, lhs_x, lhs_p, level_own, level_all,
    cube, stacked_a, stacked_b, picks, sums, beam_out, c_low, s_low, c_high, s_high, count_pad,
    l_send, l_recv, r_send, r_recv, h_send, h_recv, b_send, b_recv,
):
    segs, stations, spread = spec_ref.shape
    half = spread // 2
    chunks = half // 2 // BINS
    tiles = stations // ROWS
    both = 2 * stations
    chips = n // 2
    far = chips // 2
    groups = chips // 4
    size = segs * stations
    depth = LEVELS * 8
    band = lax.axis_index("band")
    me = lax.axis_index("blk")
    core = me % 2
    chip = me // 2
    place = place_of(chip, chips, snake)
    left = chip_of((place + chips - 1) % chips, chips, snake) * 2
    right = chip_of((place + 1) % chips, chips, snake) * 2
    sibling = chip * 2 + 1 - core

    counting = pltpu.make_async_copy(count_hbm, count_ref, count_sem)
    counting.start()
    barrier = pltpu.get_barrier_semaphore()
    for other in (left, left + 1, right, right + 1, sibling):
        pl.semaphore_signal(
            barrier, inc=1, device_id=(band, other), device_id_type=pl.DeviceIdType.MESH
        )

    def remote(src, dst, send, recv, other):
        return pltpu.make_async_remote_copy(
            src_ref=src, dst_ref=dst, send_sem=send, recv_sem=recv,
            device_id=(band, other), device_id_type=pl.DeviceIdType.MESH,
        )

    def rows_of(c):
        return pl.ds(0, 128 if c == 0 else size)

    def swap_copy(c, q):
        return remote(
            out_half.at[c, rows_of(c)], gathered.at[c, 0, q, rows_of(c)],
            h_send.at[c], h_recv.at[c], sibling,
        )

    def first_copies(c, q):
        same, cross = (gathered.at[c, 0, core, rows_of(c)], out_half.at[c, rows_of(c)])
        copies = []
        for other, slot, send, recv in (
            (left, 1, l_send, l_recv), (right, chips - 1, r_send, r_recv)
        ):
            for k, src in enumerate((same, cross)):
                which = core if k == 0 else 1 - core
                copies.append(remote(
                    src, gathered.at[c, slot, q, rows_of(c)],
                    send.at[c, 0, k], recv.at[c, 0, q], other + which,
                ))
        return copies

    def arrived_first(c):
        for slot, recv, send, other in (
            (1, l_recv, l_send, left), (chips - 1, r_recv, r_send, right)
        ):
            for q in range(2):
                remote(
                    out_half.at[c, rows_of(c)], gathered.at[c, slot, q, rows_of(c)],
                    send.at[c, 0, q], recv.at[c, 0, q], other,
                ).wait_recv()

    def ring(c, hop, last, first):
        rows = pl.ds(0, 128 if first else size)
        lq = pl.ds(0, 1) if last else pl.ds(0, 2)
        rq = pl.ds(1, 1) if last else pl.ds(0, 2)
        a = remote(
            gathered.at[c, hop - 1, lq, rows], gathered.at[c, hop, lq, rows],
            l_send.at[c, hop - 1, 0], l_recv.at[c, hop - 1, 0], left + core,
        )
        b = remote(
            gathered.at[c, chips - hop + 1, rq, rows], gathered.at[c, chips - hop, rq, rows],
            r_send.at[c, hop - 1, 0], r_recv.at[c, hop - 1, 0], right + core,
        )
        return a, b

    def ring_do(c, hop, what):
        def go(last, first):
            def fn():
                for copy in ring(c, hop, last, first):
                    getattr(copy, what)()
            return fn
        if isinstance(c, int) and isinstance(hop, int):
            go(hop == far, c == 0)()
            return
        for last in (False, True):
            for first in (False, True):
                right_hop = (hop == far) if last else (hop < far)
                right_part = (c == 0) if first else (c > 0)
                pl.when(right_hop & right_part)(go(last, first))

    def advance(c, hop):
        if isinstance(hop, int) and hop == 1:
            arrived_first(c)
        else:
            ring_do(c, hop, "wait_recv")
        when(hop < far, lambda: ring_do(c, hop + 1, "start"))

    lane24 = lane_ids(stations)
    low24 = lane24 < 64

    def piece(s, c, which):
        at = pl.multiple_of(which * (half // 2) + (c // 2) * LANES, LANES)
        re = spec_ref[s, :, pl.ds(at, LANES)].astype(F32)
        im = spec_ref[s, :, pl.ds(half + at, LANES)].astype(F32)
        if c % 2 == 0:
            return jnp.where(low24, re, pltpu.roll(im, 64, 1))
        return jnp.where(low24, pltpu.roll(re, 64, 1), im)

    count_pad[...] = jnp.zeros_like(count_pad)
    counting.wait()
    count_pad[0:segs, 0:stations] = count_ref[...].astype(F32)
    counted = count_pad[...].T
    seg24 = (lane24 & 7) >> 1
    plane = jnp.zeros((stations, LANES), F32)
    for s in range(segs):
        plane = jnp.where(seg24 == s, counted[:stations, s : s + 1], plane)
    pad = jnp.zeros((128 - size - stations, LANES), F32)

    for c in range(chunks):
        away = [piece(s, c, 1 - core) for s in range(segs)]
        home = [piece(s, c, core) for s in range(segs)]
        if c == 0:
            away += [plane, pad]
            home += [plane, pad]
        out_half[c, rows_of(c), :] = jnp.concatenate(away, 0).astype(BF16)
        gathered[c, 0, core, rows_of(c), :] = jnp.concatenate(home, 0).astype(BF16)
        if c == 0:
            pl.semaphore_wait(barrier, 5)
        swap_copy(c, core).start()
        for copy in first_copies(c, core):
            copy.start()

    low = row_ids(16, LAG)
    c_low[...], s_low[...] = cos_sin(low, 16)
    high = row_ids(half // 16, LAG) * 16
    c_high[...], s_high[...] = cos_sin(high, half // 16)

    def table_rows(h, carry):
        a = c_high[pl.ds(h, 1), :]
        b = s_high[pl.ds(h, 1), :]
        at = (h // 2) * 64 + (h % 2) * 16
        table_ref[pl.ds(pl.multiple_of(at, 16), 16), :] = (
            a * c_low[...] - b * s_low[...]
        ).astype(BF16)
        table_ref[pl.ds(pl.multiple_of(at + 32, 16), 16), :] = (
            b * c_low[...] + a * s_low[...]
        ).astype(BF16)
        return carry

    lax.fori_loop(0, half // 16, table_rows, 0, unroll=2)

    def sum_picks(e):
        lane = lax.broadcasted_iota(jnp.int32, (LANES, ROWS * n), 0)
        col = lax.broadcasted_iota(jnp.int32, (LANES, ROWS * n), 1)
        d = (lane >> 4) & 3
        off = jnp.where(
            d == 0, (chips - 2 * e) % chips,
            jnp.where(d == 1, 2 * e + 1, jnp.where(d == 2, chips - 2 * e - 1, 2 * e + 2)),
        )
        where = place + off
        where = jnp.where(where >= chips, where - chips, where)
        block = 2 * chip_of(where, chips, snake) + ((lane >> 3) & 1)
        low = lane < 64
        for q in range(2):
            k = block - (2 * chip + q)
            k = jnp.where(k < 0, k + n, k)
            for u in range(ROWS):
                hit = col == u * n + k
                at = slice(u * LANES, (u + 1) * LANES)
                picks[2 * (e % 2) + q, at, : ROWS * n] = jnp.where(hit & low, 1.0, 0.0).astype(BF16)
                picks[2 * (e % 2) + q, at, ROWS * n :] = jnp.where(hit & ~low, 1.0, 0.0).astype(BF16)

    sums[...] = jnp.zeros_like(sums)
    stacked_b[...] = jnp.zeros_like(stacked_b)

    lane8 = lane_ids(ROWS)
    lane48 = lane_ids(both)
    row128 = row_ids(LANES)

    def wait_swap(c):
        remote(
            out_half.at[c, rows_of(c)], gathered.at[c, 0, 1 - core, rows_of(c)],
            h_send.at[c], h_recv.at[c], sibling,
        ).wait_recv()

    def eight(c, slot, q, row):
        base = row // 16 * 16
        return gathered[c, slot, q, pl.ds(base, 16), :].astype(F32)[row - base : row - base + 8]

    def own_rows(c, start):
        return jnp.concatenate(
            [eight(c, 0, q, start + t * ROWS) for t in range(tiles) for q in range(2)], 0
        )

    for c in range(chunks):
        wait_swap(c)
    own_count = own_rows(0, size)
    levels = jnp.where(own_count >= ((lane48 >> 3) + 1).astype(F32), 1.0, 0.0)
    level_own[...] = jnp.concatenate([levels, levels], 0)

    def prepare_own(c):
        planes = [own_rows(c, s * stations) for s in range(segs)]
        seg8 = (lane8 & 7) >> 1
        part8 = lane8 & 1
        sign = (1 - 2 * part8).astype(F32)
        swap = lane8 ^ 1
        for g in range(BINS // 16):
            at = part8 * 64 + g * 16 + (lane8 >> 3)
            parts = [[], [], [], []]
            for r in range(0, both, ROWS):
                re = None
                for s in range(segs):
                    v = jnp.take_along_axis(planes[s][r : r + ROWS], at, axis=1)
                    re = v if s == 0 else jnp.where(seg8 == s, v, re)
                im = jnp.take_along_axis(re, swap, axis=1) * sign
                inv = lax.rsqrt(re * re + im * im + 0.25)
                parts[0].append(re)
                parts[1].append(im)
                parts[2].append(re * inv)
                parts[3].append(im * inv)
            own[g] = jnp.concatenate(parts[0] + parts[1] + parts[2] + parts[3], 0).astype(BF16)

        source = row_ids(LANES, 2 * LANES)
        column = lax.broadcasted_iota(jnp.int32, (LANES, 2 * LANES), 1)
        wanted = (column & 7) + 8 * (column >> 7)

        def spread_one(g, carry):
            for f in range(0, 16, 2):
                copy = jnp.where(source == wanted + 8 * f, 1.0, 0.0).astype(BF16)
                wide = jnp.dot(own[g], copy, preferred_element_type=F32)
                for x in range(2):
                    for k, lhs in enumerate((lhs_x, lhs_p)):
                        part = wide[k * 2 * both : (k + 1) * 2 * both, x * LANES : (x + 1) * LANES]
                        lhs[c, g * 16 + f + x] = (part * level_own[...]).astype(BF16)
            return carry

        lax.fori_loop(0, BINS // 16, spread_one, 0, unroll=True)

    def slots_of(e):
        return ((chips - 2 * e) % chips, 2 * e + 1, chips - 2 * e - 1, 2 * e + 2)

    def stack(c, e, start, part):
        slots = slots_of(e)
        rows = [
            eight(c, slots[d], q, start + t * ROWS)
            for t in ((0, 1) if part == 0 else (2,)) for d in range(4) for q in range(2)
        ]
        if part == 1:
            rows.append(jnp.zeros((64, LANES), F32))
        return jnp.concatenate(rows, 0).T

    def prepare_group(e):
        sum_picks(e)
        for v in range(2):
            turned = stack(0, e, size, v)
            level_all[:, v * LANES : (v + 1) * LANES] = jnp.where(
                turned >= ((row128 >> 3) + 1).astype(F32), 1.0, 0.0
            )[:depth].astype(BF16)
            total = jnp.zeros((both, LANES), F32)
            mine = own_rows(0, size)
            for s in range(segs):
                total = total + jnp.minimum(mine[:, 2 * s : 2 * s + 1], turned[2 * s : 2 * s + 1, :])
            total = jnp.maximum(total, 1.0)
            share = 1.0 / total
            cube[:, v * LANES : (v + 1) * LANES] = share * share * share

    def prepare_all(c, e):
        for s in range(segs):
            for v in range(2):
                turned = stack(c, e, s * stations, v)
                re, im = turned[:64], turned[64:]
                inv = lax.rsqrt(re * re + im * im + 0.25)
                x_rows[v, (2 * s) * XROWS : (2 * s) * XROWS + 64, :] = re
                x_rows[v, (2 * s + 1) * XROWS : (2 * s + 1) * XROWS + 64, :] = im
                p_rows[v, (2 * s) * XROWS : (2 * s) * XROWS + 64, :] = re * inv
                p_rows[v, (2 * s + 1) * XROWS : (2 * s + 1) * XROWS + 64, :] = im * inv

    low48 = lane48 < 64

    def one_bin(c, at):
        products = []
        for lhs, rows in ((lhs_x, x_rows), (lhs_p, p_rows)):
            cols = []
            for v in range(2):
                x8 = rows[v, pl.ds(at, 8, stride=XROWS), :]
                x16 = jnp.concatenate([x8, x8], 0).astype(BF16)
                cols.append(jnp.concatenate(
                    [x16 * level_all[k : k + 16, v * LANES : (v + 1) * LANES] for k in range(0, depth, 16)], 0
                ))
            products.append(jnp.dot(
                lhs[c, at, :, :depth], jnp.concatenate(cols, 1), preferred_element_type=F32
            ))
        cross, coh = products
        hr, hi = coh[:both], coh[both:]
        factor = (hr * hr + hi * hi) * cube[...]
        sums = []
        for part in (cross[:both] * factor, cross[both:] * factor):
            total = part[:, :LANES] + part[:, LANES:]
            sums.append(total + pltpu.roll(total, 64, 1))
        return sums

    def two_bins(c, at, stacked):
        first = one_bin(c, at)
        second = one_bin(c, at + PAIRS)
        for part in range(2):
            stacked[pl.ds(part * PAIRS + at, both, stride=ZROWS), :] = jnp.where(
                low48, first[part], second[part]
            )

    def beam_copy(c, h):
        return remote(beam_out.at[c], beam_ref.at[h, c], b_send.at[c], b_recv.at[c], sibling)

    def reduce_beams(c, e, stacked):
        wide = ROWS * n
        for o in range(2):
            q = core if o == 0 else 1 - core
            z = jnp.concatenate([
                jnp.concatenate([
                    stacked[
                        pl.ds(pl.multiple_of((t * 16 + q * 8 + u) * ZROWS, 8), 2 * PAIRS), :
                    ].astype(BF16)
                    for u in range(ROWS)
                ], 1)
                for t in range(tiles)
            ], 0)
            sums[c, o] = sums[c, o] + jnp.dot(z, picks[2 * (e % 2) + q], preferred_element_type=F32)

    def finish(c, e):
        wide = ROWS * n

        def send():
            for o in range(2):
                for t in range(tiles):
                    rows = slice(t * 2 * PAIRS, (t + 1) * 2 * PAIRS)
                    turned = jnp.concatenate(
                        [sums[c, o, rows, :wide], sums[c, o, rows, wide:]], 0
                    ).T.astype(BF16)
                    at = pl.ds(t * wide, wide)
                    if o == 0:
                        beam_ref[core, c, at, :] = turned
                    else:
                        beam_out[c, at, :] = turned
            beam_copy(c, core).start()

        when(e == groups - 1, send)

    for c in range(chunks):
        prepare_own(c)
        if c > 0:
            advance(c - 1, 1)
    advance(chunks - 1, 1)
    advance(0, 2)

    def work(step, now, before):
        e = step // chunks
        c = step % chunks

        @pl.when(c == 0)
        def _():
            prepare_group(e)

        def forward(index):
            @pl.when(index < far * chunks)
            def _():
                advance(index % chunks, index // chunks + 1)

        forward(chunks + 1 + 2 * step)
        prepare_all(c, e)
        last = jnp.maximum(step - 1, 0)
        reduce_beams(last % chunks, last // chunks, before)
        for f in range(PAIRS):
            two_bins(c, f, now)
        forward(chunks + 2 + 2 * step)
        finish(last % chunks, last // chunks)

    def double(x, carry):
        work(2 * x, stacked_a, stacked_b)
        work(2 * x + 1, stacked_b, stacked_a)
        return carry

    lax.fori_loop(0, groups * chunks // 2, double, 0)
    reduce_beams(chunks - 1, groups - 1, stacked_b)
    finish(chunks - 1, groups - 1)

    for c in range(chunks):
        swap_copy(c, core).wait_send()
        for copy in first_copies(c, core):
            copy.wait_send()

    def drain(index, carry):
        ring_do(index % chunks, index // chunks + 2, "wait_send")
        return carry

    lax.fori_loop(0, (far - 1) * chunks, drain, 0)
    for c in range(chunks):
        beam_copy(c, core).wait_send()
        beam_copy(c, 1 - core).wait_recv()


def pair_beams(spectra, counts, n, snake):
    segs, stations, spread = spectra.shape
    half = spread // 2
    chunks = half // 2 // BINS
    chips = n // 2
    far = chips // 2
    tiles = stations // ROWS
    both = 2 * stations
    dma = pltpu.SemaphoreType.DMA
    pairs = n * stations * stations * half
    return pl.pallas_call(
        functools.partial(pair_kernel, n, snake),
        out_shape=(
            jax.ShapeDtypeStruct((2, chunks, stations * n, LANES), BF16),
            jax.ShapeDtypeStruct((spread, LAG), BF16),
        ),
        in_specs=[pl.BlockSpec(memory_space=pltpu.VMEM), pl.BlockSpec(memory_space=pl.ANY)],
        out_specs=[pl.BlockSpec(memory_space=pltpu.VMEM)] * 2,
        scratch_shapes=[
            pltpu.VMEM((segs, stations), jnp.int32),
            dma(()),
            pltpu.VMEM((chunks, chips, 2, 128, LANES), BF16),
            pltpu.VMEM((chunks, 128, LANES), BF16),
            pltpu.VMEM((2, 8 * XROWS, LANES), F32),
            pltpu.VMEM((2, 8 * XROWS, LANES), F32),
            pltpu.VMEM((BINS // 16, 4 * both, LANES), BF16),
            pltpu.VMEM((chunks, BINS, 2 * both, LANES), BF16),
            pltpu.VMEM((chunks, BINS, 2 * both, LANES), BF16),
            pltpu.VMEM((2 * both, LANES), F32),
            pltpu.VMEM((LEVELS * 8, 2 * LANES), BF16),
            pltpu.VMEM((both, 2 * LANES), F32),
            pltpu.VMEM((both * ZROWS, LANES), F32),
            pltpu.VMEM((both * ZROWS, LANES), F32),
            pltpu.VMEM((4, ROWS * LANES, 2 * ROWS * n), BF16),
            pltpu.VMEM((chunks, 2, tiles * 2 * PAIRS, 2 * ROWS * n), F32),
            pltpu.VMEM((chunks, stations * n, LANES), BF16),
            pltpu.VMEM((16, LAG), F32), pltpu.VMEM((16, LAG), F32),
            pltpu.VMEM((half // 16, LAG), F32), pltpu.VMEM((half // 16, LAG), F32),
            pltpu.VMEM((LANES, LANES), F32),
            dma((chunks, far, 2)), dma((chunks, far, 2)), dma((chunks, far, 2)), dma((chunks, far, 2)),
            dma((chunks,)), dma((chunks,)), dma((chunks,)), dma((chunks,)),
        ],
        compiler_params=pltpu.CompilerParams(
            collective_id=0, has_side_effects=True, vmem_limit_bytes=(30 + n * 3 // 8) * 1024 * 1024
        ),
        cost_estimate=pl.CostEstimate(
            flops=66 * pairs, bytes_accessed=2 * spectra.size, transcendentals=0
        ),
        name="pair_beams",
    )(spectra, counts)


def lag_kernel(beam_ref, table_ref, out_ref, block_ref, sems):
    halves, chunks, rows, _ = beam_ref.shape
    copies = []
    for x in range(rows // LANES):
        at = pl.ds(x * LANES, LANES)
        beams = jnp.concatenate(
            [beam_ref[h, c, at, :] for h in range(halves) for c in range(chunks)], 1
        )
        trace = jnp.dot(beams, table_ref[...], preferred_element_type=F32)
        values = trace.astype(BF16).astype(F32)
        scale = jnp.sqrt(jnp.mean(values * values, -1, keepdims=True) + 1e-06)
        block_ref[at, :] = (values / scale).astype(BF16)
        copy = pltpu.make_async_copy(block_ref.at[at], out_ref.at[at], sems.at[x])
        copy.start()
        copies.append(copy)
    for copy in copies:
        copy.wait()


def lag_traces(beams, table):
    rows = beams.shape[2]
    return pl.pallas_call(
        lag_kernel,
        out_shape=jax.ShapeDtypeStruct((rows, LAG), BF16),
        in_specs=[pl.BlockSpec(memory_space=pltpu.VMEM)] * 2,
        out_specs=pl.BlockSpec(memory_space=pl.ANY),
        scratch_shapes=[
            pltpu.VMEM((rows, LAG), BF16), pltpu.SemaphoreType.DMA((rows // LANES,)),
        ],
        compiler_params=pltpu.CompilerParams(vmem_limit_bytes=32 * 1024 * 1024),
        name="lag_traces",
    )(beams, table)


def shards(snake, spectra, counts):
    n = lax.axis_size("blk")
    stations, segs, spread = spectra.shape
    beams, table = pair_beams(spectra.transpose(1, 0, 2), counts.T, n, snake)
    out = lag_traces(beams, table)
    return out.reshape(stations, n, LAG)


def solution(mesh):
    snake = mesh.shape["blk"] == 16
    return jax.shard_map(
        functools.partial(shards, snake),
        mesh=mesh,
        in_specs=(P(("band", "blk"), None, None), P(("band", "blk"), None)),
        out_specs=P(("band", "blk"), None, None),
        check_vma=False,
    )
```
